256 devices in a mesh: kern: 2 (over core), ty: 16 (over x, z_hi), tx: 8 (over z_lo, y).
Axes of the slice: x: 4, y: 4, z: 8 (z_hi: 4, z_lo: 2; z = z_hi * 2 + z_lo), core: 2. Of those that a mesh axis runs over, the one named last changes fastest.
Arguments:
- mask: float32 [4096, 2048], P('ty', 'tx'), may hold values from -1 to 1
- target: int32 [4096, 2048], P('ty', 'tx'), may hold values 0 or 1
- spectra: float32 [2, 24, 128, 128], P(None, 'kern'), may hold values from -4.5 to 4.5
Outputs:
- resist: float32 [4096, 2048], P('ty', 'tx')
- mask_grad: float32 [4096, 2048], P('ty', 'tx')
The draws below stay inside these ranges and needn't reach their ends.
All inputs are finite; a program needn't handle non-finite values. No bound on the sum of `target` on one device may be relied on, other than what follows from the above.
Results may differ from the reference program's by a relative error of at most 0.0003.
Values sent between devices are 32-bit elements; how exact they have to be, the bound alone decides.
A program may use at most 64 MiB of HBM per device.

```python
import math
import jax
import jax.numpy as jnp
from jax import lax

TILE = 256
HALO = 64
BAND = 128
KERNELS = 24
NY = 4096
NX = 2048


def with_ends(drawn, rng, low, largest):
    spot = [jax.random.randint(jax.random.fold_in(rng, axis), (), 0, length) for axis, length in enumerate(drawn.shape)]
    longest = drawn.shape.index(max(drawn.shape))
    beside = spot[:longest] + [(spot[longest] + 1) % drawn.shape[longest]] + spot[longest + 1:]
    return drawn.at[tuple(spot)].set(low).at[tuple(beside)].set(largest)


def steps_of(stream_key, dims, pieces, low, top_value):
    level = 1.0
    for position, parts in pieces:
        heights = jax.random.uniform(jax.random.fold_in(jax.random.fold_in(stream_key, 6), position), (parts,), jnp.float32, low / len(pieces), top_value / len(pieces))
        level = level * jnp.repeat(jnp.exp(heights), dims[position] // parts).reshape((-1,) + (1,) * (len(dims) - 1 - position))
    return level


def normal_values(stream_key, dims, spread, most, pieces=(), kind=jnp.bfloat16):
    gain = steps_of(stream_key, dims, pieces, -0.22, 0.18) if pieces else 1.0
    array = jax.random.normal(stream_key, dims, jnp.float32) * spread * gain
    return jnp.minimum(jnp.maximum(array, -most), most).astype(kind)


def setup_inputs(seed: int = 0) -> dict:
    seeds = jax.random.split(jax.random.key(seed), 4)
    mask = jnp.clip(jax.random.uniform(seeds[0], (NY, NX), jnp.float32, -1.0, 1.0) * steps_of(seeds[0], (NY, NX), ((0, 16), (1, 8)), -0.4, 0.0), -1.0, 1.0)
    target = with_ends((jax.random.randint(seeds[1], (NY, NX), 0, 2) < 1).astype(jnp.int32), jax.random.fold_in(seeds[1], 1), 0, 1)
    spectra = normal_values(seeds[2], (2, KERNELS, BAND, BAND), 0.75, 4.5, ((1, 2),), jnp.float32)
    return dict(mask=mask, target=target, spectra=spectra)


STEEP = 8.0
LEVEL = 1.0


def matmul(pattern, first, second):
    return jnp.einsum(pattern, first.astype(jnp.float32), second.astype(jnp.float32), precision=lax.Precision.HIGHEST, preferred_element_type=jnp.float32)


def make_tables(band_size, window_size, tile_size, margin):
    frequency = jnp.arange(band_size, dtype=jnp.int32) - band_size // 2
    positions = jnp.arange(window_size, dtype=jnp.int32)
    centred = jnp.arange(tile_size, dtype=jnp.int32) + margin
    angle_unit = 2.0 * math.pi / window_size
    outer_angle = jnp.mod(frequency[:, None] * positions[None, :], window_size).astype(jnp.float32) * angle_unit
    inner_angle = jnp.mod(centred[:, None] * frequency[None, :], window_size).astype(jnp.float32) * angle_unit
    return jnp.cos(outer_angle), -jnp.sin(outer_angle), jnp.cos(inner_angle), jnp.sin(inner_angle)


def window_spectrum(windows, tables):
    fwd_re, fwd_im, inv_re, inv_im = tables
    half_re = matmul("uy,tyx->tux", fwd_re, windows)
    half_im = matmul("uy,tyx->tux", fwd_im, windows)
    spec_re = matmul("tux,vx->tuv", half_re, fwd_re) - matmul("tux,vx->tuv", half_im, fwd_im)
    spec_im = matmul("tux,vx->tuv", half_re, fwd_im) + matmul("tux,vx->tuv", half_im, fwd_re)
    return spec_re, spec_im


def kernel_fields(spec_re, spec_im, kern_re, kern_im, tables, scale):
    fwd_re, fwd_im, inv_re, inv_im = tables
    prod_re = spec_re[:, None] * kern_re[None] - spec_im[:, None] * kern_im[None]
    prod_im = spec_re[:, None] * kern_im[None] + spec_im[:, None] * kern_re[None]
    rows_re = matmul("yu,tkuv->tkyv", inv_re, prod_re) - matmul("yu,tkuv->tkyv", inv_im, prod_im)
    rows_im = matmul("yu,tkuv->tkyv", inv_re, prod_im) + matmul("yu,tkuv->tkyv", inv_im, prod_re)
    field_re = (matmul("tkyv,xv->tkyx", rows_re, inv_re) - matmul("tkyv,xv->tkyx", rows_im, inv_im)) * scale
    field_im = (matmul("tkyv,xv->tkyx", rows_re, inv_im) + matmul("tkyv,xv->tkyx", rows_im, inv_re)) * scale
    return field_re, field_im


def resist_terms(intensity, goal):
    resist = jax.nn.sigmoid(STEEP * (intensity - LEVEL))
    weight = 2.0 * (resist - goal.astype(jnp.float32)) * STEEP * resist * (1.0 - resist)
    return resist, weight


def back_spectrum(weight, field_re, field_im, kern_re, kern_im, tables, scale):
    fwd_re, fwd_im, inv_re, inv_im = tables
    load_re = weight[:, None] * field_re
    load_im = weight[:, None] * field_im
    cols_re = matmul("tkyx,xv->tkyv", load_re, inv_re) + matmul("tkyx,xv->tkyv", load_im, inv_im)
    cols_im = matmul("tkyx,xv->tkyv", load_im, inv_re) - matmul("tkyx,xv->tkyv", load_re, inv_im)
    spread_re = matmul("yu,tkyv->tkuv", inv_re, cols_re) + matmul("yu,tkyv->tkuv", inv_im, cols_im)
    spread_im = matmul("yu,tkyv->tkuv", inv_re, cols_im) - matmul("yu,tkyv->tkuv", inv_im, cols_re)
    back_re = jnp.sum(kern_re[None] * spread_re + kern_im[None] * spread_im, axis=1) * scale
    back_im = jnp.sum(kern_re[None] * spread_im - kern_im[None] * spread_re, axis=1) * scale
    return back_re, back_im


def window_gradient(back_re, back_im, tables):
    fwd_re, fwd_im, inv_re, inv_im = tables
    lift_re = matmul("uy,tuv->tyv", fwd_re, back_re) + matmul("uy,tuv->tyv", fwd_im, back_im)
    lift_im = matmul("uy,tuv->tyv", fwd_re, back_im) - matmul("uy,tuv->tyv", fwd_im, back_re)
    return 2.0 * (matmul("tyv,vx->tyx", lift_re, fwd_re) + matmul("tyv,vx->tyx", lift_im, fwd_im))


def reference(mask, target, spectra):
    window_size = TILE + 2 * HALO
    tables = make_tables(BAND, window_size, TILE, HALO)
    scale = 1.0 / (window_size * window_size)
    widened = jnp.pad(mask, HALO)
    tile_rows = NY // TILE
    tile_cols = NX // TILE
    kern_re = spectra[0]
    kern_im = spectra[1]

    def one_tile(number):
        number = number.astype(jnp.int32)
        row_at = ((number // tile_cols) * TILE).astype(jnp.int32)
        col_at = ((number % tile_cols) * TILE).astype(jnp.int32)
        window = lax.dynamic_slice(widened, (row_at, col_at), (window_size, window_size))[None]
        goal = lax.dynamic_slice(target, (row_at, col_at), (TILE, TILE))[None]
        spec_re, spec_im = window_spectrum(window, tables)
        field_re, field_im = kernel_fields(spec_re, spec_im, kern_re, kern_im, tables, scale)
        intensity = jnp.sum(field_re * field_re + field_im * field_im, axis=1)
        resist, weight = resist_terms(intensity, goal)
        back_re, back_im = back_spectrum(weight, field_re, field_im, kern_re, kern_im, tables, scale)
        return resist[0], window_gradient(back_re, back_im, tables)[0]

    numbers = jnp.arange(tile_rows * tile_cols, dtype=jnp.int32)
    resist_tiles, grad_tiles = lax.map(one_tile, numbers)
    resist = resist_tiles.reshape(tile_rows, tile_cols, TILE, TILE).transpose(0, 2, 1, 3).reshape(NY, NX)

    def place(number, total):
        number = jnp.asarray(number).astype(jnp.int32)
        row_at = ((number // tile_cols) * TILE).astype(jnp.int32)
        col_at = ((number % tile_cols) * TILE).astype(jnp.int32)
        current = lax.dynamic_slice(total, (row_at, col_at), (window_size, window_size))
        return lax.dynamic_update_slice(total, current + grad_tiles[number], (row_at, col_at))

    total = lax.fori_loop(0, tile_rows * tile_cols, place, jnp.zeros(widened.shape, jnp.float32))
    return resist, total[HALO:HALO + NY, HALO:HALO + NX]
```

```python
import math

import jax
import jax.numpy as jnp
import numpy as np
from jax import lax
from jax.experimental import pallas as pl
from jax.experimental.pallas import tpu as pltpu
from jax.sharding import PartitionSpec as P

TILE = 256
HALO = 64
BAND = 128
WINDOW = TILE + 2 * HALO
HALF = TILE // 2
STEEP = 8.0
LEVEL = 1.0
UNROLL = 2
SCALE = 1.0 / (WINDOW * WINDOW)
MESH = pl.DeviceIdType.MESH
F32 = jnp.float32
BF16 = jnp.bfloat16


def halves(table):
    table = np.asarray(table, np.float32)
    hi = table.astype(BF16)
    lo = (table - hi.astype(np.float32)).astype(BF16)
    return hi, lo


def make_tables():
    freq = np.arange(BAND) - BAND // 2
    order = np.concatenate(
        [np.arange(TILE) + HALO, np.arange(HALO), np.arange(HALO) + HALO + TILE]
    )
    angle = np.mod(order[:, None] * freq[None, :], WINDOW).astype(np.float64) * (2.0 * math.pi / WINDOW)
    c, s = np.cos(angle), np.sin(angle)
    by_place = np.concatenate([c, -s, s, c], 1)
    by_freq = np.block([[c.T, s.T], [-s.T, c.T]])
    return np.stack(halves(by_place)), np.stack(halves(by_freq))


def split(x):
    hi = x.astype(BF16)
    return hi, (x - hi.astype(F32)).astype(BF16)


def dot(a, b):
    return jnp.dot(a, b, preferred_element_type=F32)


def rows_by_table(x, table):
    hi, lo = split(x)
    t_hi, t_lo = table
    left = jnp.concatenate([hi, lo, hi], axis=1)
    return dot(left, jnp.concatenate([t_hi, t_hi, t_lo], axis=0))


def table_by_rows(table, hi, lo):
    t_hi, t_lo = table
    left = jnp.concatenate([t_hi, t_hi, t_lo], axis=1)
    return dot(left, jnp.concatenate([hi, lo, hi], axis=0))


def fold(a, b):
    left_lanes = lax.broadcasted_iota(jnp.int32, a.shape, 1) < HALO
    first = jnp.where(left_lanes, a, pltpu.roll(b, HALO, 1))
    second = jnp.where(left_lanes, pltpu.roll(a, HALO, 1), b)
    return first, second


def body(
    mask_h, target_h, spec_h, place_h, freq_h,
    resist_h, grad_h,
    mask_v, target_v, spec_v, place_v, freq_v,
    send_side, send_diag, got_v, got_side, got_diag,
    acc_half, a_stack, f_part, f_got, r_stack, field, inten, inten_got, weight, resist_v,
    c_stack, w_part, w_got, g_v, g_side, g_diag, gg_v, gg_side, gg_diag, out_half,
    load_sem, store_sem, h_send, h_recv, p_send, p_recv, g_send, g_recv,
):
    kern, ty, tx = lax.axis_index("kern"), lax.axis_index("ty"), lax.axis_index("tx")
    n_ty, n_tx = lax.axis_size("ty"), lax.axis_size("tx")
    other = 1 - kern
    vt = ty - 1 + 2 * kern
    has_v = jnp.logical_and(vt >= 0, vt < n_ty)
    has_l, has_r = tx > 0, tx < n_tx - 1
    has_dl, has_dr = jnp.logical_and(has_v, has_l), jnp.logical_and(has_v, has_r)
    partner = (other, ty, tx)
    vertical = (other, vt, tx)
    left, right = (kern, ty, tx - 1), (kern, ty, tx + 1)
    diag_l, diag_r = (other, vt, tx - 1), (other, vt, tx + 1)
    peers = [(has_v, vertical), (has_l, left), (has_r, right), (has_dl, diag_l), (has_dr, diag_r)]

    barrier = pltpu.get_barrier_semaphore()
    pl.semaphore_signal(barrier, inc=1, device_id=partner, device_id_type=MESH)
    for has, peer in peers:

        @pl.when(has)
        def _(peer=peer):
            pl.semaphore_signal(barrier, inc=1, device_id=peer, device_id_type=MESH)

    loads = [
        (mask_h, mask_v), (place_h, place_v), (freq_h, freq_v), (spec_h, spec_v), (target_h, target_v),
    ]
    loads = [pltpu.make_async_copy(a, b, load_sem.at[i]) for i, (a, b) in enumerate(loads)]
    for load in loads:
        load.start()
    l_mask, l_place, l_freq, l_spec, l_target = loads

    def place(rows, lanes):
        return place_v[0, rows, lanes], place_v[1, rows, lanes]

    def inverse_lanes(part):
        both = jnp.concatenate([freq_v[part, :, :TILE], freq_v[part, :, WINDOW : WINDOW + TILE]], axis=1)
        return both

    def block_of(first, second, axis):
        return tuple(jnp.concatenate([a, b], axis=axis) for a, b in zip(first, second))

    inner, direct, turned = slice(0, TILE), slice(0, TILE), slice(TILE, 2 * TILE)
    edges = slice(TILE, WINDOW)

    a_stack[...] = jnp.zeros(a_stack.shape, BF16)
    for has, bufs in (
        (has_v, (got_v, gg_v)),
        (has_l, (got_side.at[0], gg_side.at[0])),
        (has_r, (got_side.at[1], gg_side.at[1])),
        (has_dl, (got_diag.at[0], gg_diag.at[0])),
        (has_dr, (got_diag.at[1], gg_diag.at[1])),
    ):

        @pl.when(jnp.logical_not(has))
        def _(bufs=bufs):
            for buf in bufs:
                buf[...] = jnp.zeros(buf.shape, F32)

    half_at = pl.multiple_of(kern * HALF, HALF)
    edge_at = pl.multiple_of(kern * (TILE - HALO), HALO)
    l_mask.wait()
    mask_half = mask_v[pl.ds(half_at, HALF), :]
    mask_edge = mask_v[pl.ds(edge_at, HALO), :]

    def side_lanes(x):
        lanes = lax.broadcasted_iota(jnp.int32, (x.shape[0], 128), 1) < HALO
        return jnp.where(lanes, x[:, :128], x[:, 128:])

    sides = side_lanes(mask_half)
    first, second = fold(sides[:64], sides[64:])
    send_side[0] = first
    send_side[1] = second
    corners = side_lanes(mask_edge)
    first, second = fold(corners[:32], corners[32:])
    send_diag[0] = first
    send_diag[1] = second

    pl.semaphore_wait(barrier, 1 + sum(has.astype(jnp.int32) for has, _ in peers))

    def remote(src, dst, send, recv, at, peer):
        return pltpu.make_async_remote_copy(
            src_ref=src, dst_ref=dst, send_sem=send.at[at], recv_sem=recv.at[at],
            device_id=peer, device_id_type=MESH,
        )

    def exchange(src_v, src_side, src_diag, dst_v, dst_side, dst_diag, send, recv):
        return [
            (has_v, has_v, remote(src_v, dst_v, send, recv, 0, vertical)),
            (has_l, has_r, remote(src_side.at[0], dst_side.at[1], send, recv, 1, left)),
            (has_r, has_l, remote(src_side.at[1], dst_side.at[0], send, recv, 2, right)),
            (has_dl, has_dr, remote(src_diag.at[0], dst_diag.at[1], send, recv, 3, diag_l)),
            (has_dr, has_dl, remote(src_diag.at[1], dst_diag.at[0], send, recv, 4, diag_r)),
        ]

    def each(copies, which, act):
        for entry in copies:

            @pl.when(entry[which])
            def _(copy=entry[2]):
                act(copy)

    halo = exchange(
        mask_v.at[pl.ds(edge_at, HALO)], send_side, send_diag, got_v, got_side, got_diag,
        h_send, h_recv,
    )
    each(halo, 0, lambda c: c.start())

    l_place.wait()
    own = place(inner, direct)
    acc_half[...] = rows_by_table(mask_half, own)
    l_freq.wait()
    each(halo, 1, lambda c: c.wait_recv())

    top, bottom = fold(got_side[0], got_side[1])
    side_part = rows_by_table(jnp.concatenate([top, bottom], axis=0), place(edges, direct))
    half_hi, half_lo = split(acc_half[...] + side_part)
    top, bottom = fold(got_diag[0], got_diag[1])
    strip = rows_by_table(got_v[...], own)
    strip = strip + rows_by_table(jnp.concatenate([top, bottom], axis=0), place(edges, direct))
    strip_hi, strip_lo = split(strip)
    edge_rows = pl.ds(pl.multiple_of(HALF + kern * HALO, HALO), HALO)
    for part, (main, edge) in enumerate(((half_hi, strip_hi), (half_lo, strip_lo))):
        a_stack[part, pl.ds(0, HALF), :] = main
        a_stack[part, edge_rows, :] = edge
    half_lanes = pl.ds(half_at, HALF)
    own_y = []
    for part in range(2):
        cos = [freq_v[part, pl.ds(0, BAND), half_lanes], freq_v[part, :BAND, TILE:WINDOW]]
        sin_lanes = pl.ds(pl.multiple_of(WINDOW + half_at, HALF), HALF)
        sin = [freq_v[part, pl.ds(0, BAND), sin_lanes], freq_v[part, :BAND, WINDOW + TILE :]]
        own_y.append(jnp.concatenate([jnp.concatenate(cos, axis=1), jnp.concatenate(sin, axis=1)], axis=0))
    full = table_by_rows(own_y, a_stack[0], a_stack[1])
    f_part[:, :BAND] = full[:BAND, :BAND] + full[BAND:, BAND:]
    f_part[:, BAND:] = full[:BAND, BAND:] - full[BAND:, :BAND]
    f_copy = remote(f_part, f_got, p_send, p_recv, 0, partner)
    f_copy.start()
    l_spec.wait()
    f_copy.wait_recv()
    w_part[...] = (f_part[...] + f_got[...]) * SCALE

    kernels = spec_v.shape[1]

    def loop(step):
        def several(i, carry):
            for j in range(UNROLL):
                step(i * UNROLL + j)
            return carry

        lax.fori_loop(0, kernels // UNROLL, several, 0)

    def to_columns(k):
        f_re, f_im = w_part[:, :BAND], w_part[:, BAND:]
        h_re, h_im = spec_v[0, k], spec_v[1, k]
        prod = jnp.concatenate([f_re * h_re - f_im * h_im, f_re * h_im + f_im * h_re], axis=1)
        hi, lo = split(rows_by_table(prod, (inverse_lanes(0), inverse_lanes(1))))
        r_stack[k, pl.ds(0, 128), :] = hi[:, :TILE]
        r_stack[k, pl.ds(128, 128), :] = hi[:, TILE:]
        r_stack[k, pl.ds(256, 128), :] = lo[:, :TILE]
        r_stack[k, pl.ds(384, 128), :] = lo[:, TILE:]

    loop(to_columns)

    i_copies = []
    for b in range(2):
        inten[b] = jnp.zeros((HALF, TILE), F32)

        def to_rows(k, b=b):
            at = slice(b * HALF, (b + 1) * HALF)
            hi, lo = r_stack[k, pl.ds(0, TILE), :], r_stack[k, pl.ds(TILE, TILE), :]
            value = table_by_rows(block_of(place(at, direct), place(at, turned), 0), hi, lo)
            field[b, k] = value
            re, im = value[:HALF], value[HALF:]
            inten[b] += re * re + im * im

        loop(to_rows)
        copy = remote(inten.at[b], inten_got.at[b], p_send, p_recv, 1 + b, partner)
        copy.start()
        i_copies.append(copy)

    l_target.wait()
    stores = []
    for b in range(2):
        i_copies[b].wait_recv()
        rows = pl.ds(b * HALF, HALF)
        resist = jax.nn.sigmoid(STEEP * (inten[b] + inten_got[b] - LEVEL))
        goal = target_v[rows, :].astype(F32)
        resist_v[rows, :] = resist
        weight[...] = 2.0 * (resist - goal) * STEEP * resist * (1.0 - resist)
        store = pltpu.make_async_copy(resist_v.at[rows], resist_h.at[rows], store_sem.at[b])
        store.start()
        stores.append(store)

        def back_columns(k, b=b):
            w = weight[...]
            load = jnp.concatenate([w * field[b, k, pl.ds(0, HALF), :], w * field[b, k, pl.ds(HALF, HALF), :]], axis=1)
            hi, lo = split(rows_by_table(load, block_of(place(inner, direct), place(inner, turned), 0)))
            c_stack[k, pl.ds(b * HALF, HALF), :] = hi
            c_stack[k, pl.ds(TILE + b * HALF, HALF), :] = lo

        loop(back_columns)

    f_copy.wait_send()
    f_part[...] = jnp.zeros((BAND, 2 * BAND), F32)

    def back_rows(k):
        hi, lo = c_stack[k, pl.ds(0, TILE), :], c_stack[k, pl.ds(TILE, TILE), :]
        value = table_by_rows([jnp.concatenate([freq_v[part, :BAND, :TILE], freq_v[part, :BAND, WINDOW : WINDOW + TILE]], axis=0) for part in range(2)], hi, lo)
        s_re = value[:BAND, :BAND] + value[BAND:, BAND:]
        s_im = value[:BAND, BAND:] - value[BAND:, :BAND]
        h_re, h_im = spec_v[0, k], spec_v[1, k]
        f_part[:, :BAND] += h_re * s_re + h_im * s_im
        f_part[:, BAND:] += h_re * s_im - h_im * s_re

    loop(back_rows)
    w_copy = remote(f_part, w_got, p_send, p_recv, 3, partner)
    w_copy.start()
    w_copy.wait_recv()

    lifted = rows_by_table((f_part[...] + w_got[...]) * (2.0 * SCALE), (freq_v[0], freq_v[1]))
    lifted = jnp.concatenate([lifted[:, :WINDOW], lifted[:, WINDOW:]], axis=0)
    hi, lo = split(lifted)
    edge_place = pl.ds(pl.multiple_of(TILE + kern * HALO, HALO), HALO)
    own_rows = place(pl.ds(half_at, HALF), direct)
    grad = table_by_rows(block_of(own_rows, place(edge_place, direct), 0), hi, lo)
    g_v[...] = grad[HALF:, :TILE]
    first, second = fold(grad[:64, TILE:], grad[64:HALF, TILE:])
    g_side[0] = first
    g_side[1] = second
    first, second = fold(grad[HALF : HALF + 32, TILE:], grad[HALF + 32 :, TILE:])
    g_diag[0] = first
    g_diag[1] = second
    margin = exchange(g_v, g_side, g_diag, gg_v, gg_side, gg_diag, g_send, g_recv)
    each(margin, 0, lambda c: c.start())
    out_half[...] = grad[:HALF, :TILE]
    each(margin, 1, lambda c: c.wait_recv())

    def added(x, lanes):
        mine = lax.broadcasted_iota(jnp.int32, lanes.shape, 1) < HALO
        zero = jnp.zeros(lanes.shape, F32)
        return x + jnp.concatenate([jnp.where(mine, lanes, zero), jnp.where(mine, zero, lanes)], axis=1)

    top, bottom = fold(gg_side[0], gg_side[1])
    out_half[...] = added(out_half[...], jnp.concatenate([top, bottom], axis=0))
    top, bottom = fold(gg_diag[0], gg_diag[1])
    near = pl.ds(pl.multiple_of(kern * HALO, HALO), HALO)
    out_half[near, :] = out_half[near, :] + added(gg_v[...], jnp.concatenate([top, bottom], axis=0))

    mine = grad_h.at[pl.ds(half_at, HALF)]
    g_copy = remote(out_half, mine, p_send, p_recv, 4, partner)
    g_copy.start()
    store = pltpu.make_async_copy(out_half, mine, store_sem.at[2])
    store.start()
    stores.append(store)

    each(halo, 0, lambda c: c.wait_send())
    each(margin, 0, lambda c: c.wait_send())
    for copy in i_copies:
        copy.wait_send()
    w_copy.wait_send()
    for store in stores:
        store.wait()
    g_copy.wait()


def on_device(mask, target, spectra):
    tables = make_tables()
    kernels = spectra.shape[1]
    vmem = lambda shape, dtype=F32: pltpu.VMEM(shape, dtype)
    dma = lambda n: pltpu.SemaphoreType.DMA((n,))
    scratch = [
        vmem((TILE, TILE)), vmem((TILE, TILE), jnp.int32), vmem(spectra.shape),
        *[vmem(t.shape, BF16) for t in tables],
        vmem((2, 64, 128)), vmem((2, 32, 128)),
        vmem((HALO, TILE)), vmem((2, 64, 128)), vmem((2, 32, 128)),
        vmem((HALF, TILE)), vmem((2, TILE, TILE), BF16),
        vmem((BAND, 2 * BAND)), vmem((BAND, 2 * BAND)),
        vmem((kernels, 2 * TILE, TILE), BF16), vmem((2, kernels, TILE, TILE)),
        vmem((2, HALF, TILE)), vmem((2, HALF, TILE)), vmem((HALF, TILE)), vmem((TILE, TILE)),
        vmem((kernels, 2 * TILE, TILE), BF16), vmem((BAND, 2 * BAND)), vmem((BAND, 2 * BAND)),
        vmem((HALO, TILE)), vmem((2, 64, 128)), vmem((2, 32, 128)),
        vmem((HALO, TILE)), vmem((2, 64, 128)), vmem((2, 32, 128)),
        vmem((HALF, TILE)),
        dma(5), dma(3), dma(5), dma(5), dma(5), dma(5), dma(5), dma(5),
    ]
    anywhere = pl.BlockSpec(memory_space=pl.ANY)
    return pl.pallas_call(
        body,
        out_shape=[jax.ShapeDtypeStruct((TILE, TILE), F32)] * 2,
        in_specs=[anywhere] * (3 + len(tables)),
        out_specs=[anywhere] * 2,
        scratch_shapes=scratch,
        compiler_params=pltpu.CompilerParams(
            collective_id=0, has_side_effects=True, vmem_limit_bytes=60 * 1024 * 1024
        ),
        name="socs_step",
    )(mask, target, spectra, *[jnp.asarray(t) for t in tables])


def solution(mesh):
    return jax.shard_map(
        on_device,
        mesh=mesh,
        in_specs=(P("ty", "tx"), P("ty", "tx"), P(None, "kern", None, None)),
        out_specs=(P("ty", "tx"), P("ty", "tx")),
        check_vma=False,
    )
```

```python
import math

import jax
import jax.numpy as jnp
import numpy as np
from jax import lax
from jax.experimental import pallas as pl
from jax.experimental.pallas import tpu as pltpu
from jax.sharding import PartitionSpec as P

TILE = 256
HALO = 64
BAND = 128
WINDOW = TILE + 2 * HALO
HALF = TILE // 2
STEEP = 8.0
LEVEL = 1.0
SCALE = 1.0 / (WINDOW * WINDOW)
MESH = pl.DeviceIdType.MESH
F32 = jnp.float32
BF16 = jnp.bfloat16


def halves(table):
    table = np.asarray(table, np.float32)
    hi = table.astype(BF16)
    lo = (table - hi.astype(np.float32)).astype(BF16)
    return hi, lo


def make_tables():
    freq = np.arange(BAND) - BAND // 2
    order = np.concatenate(
        [np.arange(TILE) + HALO, np.arange(HALO), np.arange(HALO) + HALO + TILE]
    )
    angle = np.mod(order[:, None] * freq[None, :], WINDOW).astype(np.float64) * (2.0 * math.pi / WINDOW)
    c, s = np.cos(angle), np.sin(angle)
    by_place = np.concatenate([c, -s, s, c], 1)
    by_freq = np.block([[c.T, s.T], [-s.T, c.T]])
    return np.stack(halves(by_place)), np.stack(halves(by_freq))


def split(x):
    hi = x.astype(BF16)
    return hi, (x - hi.astype(F32)).astype(BF16)


def dot(a, b):
    return jnp.dot(a, b, preferred_element_type=F32)


def rows_by_table(x, table):
    hi, lo = split(x)
    t_hi, t_lo = table
    left = jnp.concatenate([hi, lo, hi], axis=1)
    return dot(left, jnp.concatenate([t_hi, t_hi, t_lo], axis=0))


def table_by_rows(table, hi, lo):
    t_hi, t_lo = table
    left = jnp.concatenate([t_hi, t_hi, t_lo], axis=1)
    return dot(left, jnp.concatenate([hi, lo, hi], axis=0))


def fold(a, b):
    left_lanes = lax.broadcasted_iota(jnp.int32, a.shape, 1) < HALO
    first = jnp.where(left_lanes, a, pltpu.roll(b, HALO, 1))
    second = jnp.where(left_lanes, pltpu.roll(a, HALO, 1), b)
    return first, second


def body(
    mask_h, target_h, spec_h, place_h, freq_h,
    resist_h, grad_h,
    mask_v, target_v, spec_v, place_v, freq_v,
    send_side, send_diag, got_v, got_side, got_diag,
    acc_half, a_stack, f_part, f_got, r_stack, field, inten, inten_got, weight, resist_v,
    c_stack, w_part, w_got, g_v, g_side, g_diag, gg_v, gg_side, gg_diag, out_half,
    load_sem, store_sem, h_send, h_recv, p_send, p_recv, g_send, g_recv,
):
    kern, ty, tx = lax.axis_index("kern"), lax.axis_index("ty"), lax.axis_index("tx")
    n_ty, n_tx = lax.axis_size("ty"), lax.axis_size("tx")
    other = 1 - kern
    vt = ty - 1 + 2 * kern
    has_v = jnp.logical_and(vt >= 0, vt < n_ty)
    has_l, has_r = tx > 0, tx < n_tx - 1
    has_dl, has_dr = jnp.logical_and(has_v, has_l), jnp.logical_and(has_v, has_r)
    partner = (other, ty, tx)
    vertical = (other, vt, tx)
    left, right = (kern, ty, tx - 1), (kern, ty, tx + 1)
    diag_l, diag_r = (other, vt, tx - 1), (other, vt, tx + 1)
    peers = [(has_v, vertical), (has_l, left), (has_r, right), (has_dl, diag_l), (has_dr, diag_r)]

    barrier = pltpu.get_barrier_semaphore()
    pl.semaphore_signal(barrier, inc=1, device_id=partner, device_id_type=MESH)
    for has, peer in peers:

        @pl.when(has)
        def _(peer=peer):
            pl.semaphore_signal(barrier, inc=1, device_id=peer, device_id_type=MESH)

    loads = [
        (mask_h, mask_v), (place_h, place_v), (freq_h, freq_v), (spec_h, spec_v), (target_h, target_v),
    ]
    loads = [pltpu.make_async_copy(a, b, load_sem.at[i]) for i, (a, b) in enumerate(loads)]
    for load in loads:
        load.start()
    l_mask, l_place, l_freq, l_spec, l_target = loads

    def place(rows, lanes):
        return place_v[0, rows, lanes], place_v[1, rows, lanes]

    def inverse_lanes(part):
        both = jnp.concatenate([freq_v[part, :, :TILE], freq_v[part, :, WINDOW : WINDOW + TILE]], axis=1)
        return both

    def block_of(first, second, axis):
        return tuple(jnp.concatenate([a, b], axis=axis) for a, b in zip(first, second))

    inner, direct, turned = slice(0, TILE), slice(0, TILE), slice(TILE, 2 * TILE)
    edges = slice(TILE, WINDOW)

    a_stack[...] = jnp.zeros(a_stack.shape, BF16)
    for has, bufs in (
        (has_v, (got_v, gg_v)),
        (has_l, (got_side.at[0], gg_side.at[0])),
        (has_r, (got_side.at[1], gg_side.at[1])),
        (has_dl, (got_diag.at[0], gg_diag.at[0])),
        (has_dr, (got_diag.at[1], gg_diag.at[1])),
    ):

        @pl.when(jnp.logical_not(has))
        def _(bufs=bufs):
            for buf in bufs:
                buf[...] = jnp.zeros(buf.shape, F32)

    half_at = pl.multiple_of(kern * HALF, HALF)
    edge_at = pl.multiple_of(kern * (TILE - HALO), HALO)
    l_mask.wait()
    mask_half = mask_v[pl.ds(half_at, HALF), :]
    mask_edge = mask_v[pl.ds(edge_at, HALO), :]

    def side_lanes(x):
        lanes = lax.broadcasted_iota(jnp.int32, (x.shape[0], 128), 1) < HALO
        return jnp.where(lanes, x[:, :128], x[:, 128:])

    sides = side_lanes(mask_half)
    first, second = fold(sides[:64], sides[64:])
    send_side[0] = first
    send_side[1] = second
    corners = side_lanes(mask_edge)
    first, second = fold(corners[:32], corners[32:])
    send_diag[0] = first
    send_diag[1] = second

    pl.semaphore_wait(barrier, 1 + sum(has.astype(jnp.int32) for has, _ in peers))

    def remote(src, dst, send, recv, at, peer):
        return pltpu.make_async_remote_copy(
            src_ref=src, dst_ref=dst, send_sem=send.at[at], recv_sem=recv.at[at],
            device_id=peer, device_id_type=MESH,
        )

    def exchange(src_v, src_side, src_diag, dst_v, dst_side, dst_diag, send, recv):
        return [
            (has_v, has_v, remote(src_v, dst_v, send, recv, 0, vertical)),
            (has_l, has_r, remote(src_side.at[0], dst_side.at[1], send, recv, 1, left)),
            (has_r, has_l, remote(src_side.at[1], dst_side.at[0], send, recv, 2, right)),
            (has_dl, has_dr, remote(src_diag.at[0], dst_diag.at[1], send, recv, 3, diag_l)),
            (has_dr, has_dl, remote(src_diag.at[1], dst_diag.at[0], send, recv, 4, diag_r)),
        ]

    def each(copies, which, act):
        for entry in copies:

            @pl.when(entry[which])
            def _(copy=entry[2]):
                act(copy)

    halo = exchange(
        mask_h.at[pl.ds(edge_at, HALO)], send_side, send_diag, got_v, got_side, got_diag,
        h_send, h_recv,
    )
    each(halo, 0, lambda c: c.start())

    l_place.wait()
    own = place(inner, direct)
    acc_half[...] = rows_by_table(mask_half, own)
    l_freq.wait()
    each(halo, 1, lambda c: c.wait_recv())

    top, bottom = fold(got_side[0], got_side[1])
    side_part = rows_by_table(jnp.concatenate([top, bottom], axis=0), place(edges, direct))
    half_hi, half_lo = split(acc_half[...] + side_part)
    top, bottom = fold(got_diag[0], got_diag[1])
    strip = rows_by_table(got_v[...], own)
    strip = strip + rows_by_table(jnp.concatenate([top, bottom], axis=0), place(edges, direct))
    strip_hi, strip_lo = split(strip)
    edge_rows = pl.ds(pl.multiple_of(HALF + kern * HALO, HALO), HALO)
    for part, (main, edge) in enumerate(((half_hi, strip_hi), (half_lo, strip_lo))):
        a_stack[part, pl.ds(0, HALF), :] = main
        a_stack[part, edge_rows, :] = edge
    half_lanes = pl.ds(half_at, HALF)
    own_y = []
    for part in range(2):
        cos = [freq_v[part, pl.ds(0, BAND), half_lanes], freq_v[part, :BAND, TILE:WINDOW]]
        sin_lanes = pl.ds(pl.multiple_of(WINDOW + half_at, HALF), HALF)
        sin = [freq_v[part, pl.ds(0, BAND), sin_lanes], freq_v[part, :BAND, WINDOW + TILE :]]
        own_y.append(jnp.concatenate([jnp.concatenate(cos, axis=1), jnp.concatenate(sin, axis=1)], axis=0))
    full = table_by_rows(own_y, a_stack[0], a_stack[1])
    f_part[:, :BAND] = full[:BAND, :BAND] + full[BAND:, BAND:]
    f_part[:, BAND:] = full[:BAND, BAND:] - full[BAND:, :BAND]
    f_copy = remote(f_part, f_got, p_send, p_recv, 0, partner)
    f_copy.start()
    l_spec.wait()
    f_copy.wait_recv()
    w_part[...] = (f_part[...] + f_got[...]) * SCALE

    kernels = spec_v.shape[1]

    def loop(step):
        for k in range(kernels):
            step(k)

    def to_columns(k):
        f_re, f_im = w_part[:, :BAND], w_part[:, BAND:]
        h_re, h_im = spec_v[0, k], spec_v[1, k]
        prod = jnp.concatenate([f_re * h_re - f_im * h_im, f_re * h_im + f_im * h_re], axis=1)
        hi, lo = split(rows_by_table(prod, (inverse_lanes(0), inverse_lanes(1))))
        r_stack[k, pl.ds(0, 128), :] = hi[:, :TILE]
        r_stack[k, pl.ds(128, 128), :] = hi[:, TILE:]
        r_stack[k, pl.ds(256, 128), :] = lo[:, :TILE]
        r_stack[k, pl.ds(384, 128), :] = lo[:, TILE:]

    loop(to_columns)

    i_copies = []
    for b in range(2):
        inten[b] = jnp.zeros((HALF, TILE), F32)

        def to_rows(k, b=b):
            at = slice(b * HALF, (b + 1) * HALF)
            hi, lo = r_stack[k, pl.ds(0, TILE), :], r_stack[k, pl.ds(TILE, TILE), :]
            value = table_by_rows(block_of(place(at, direct), place(at, turned), 0), hi, lo)
            field[b, k] = value
            re, im = value[:HALF], value[HALF:]
            inten[b] += re * re + im * im

        loop(to_rows)
        copy = remote(inten.at[b], inten_got.at[b], p_send, p_recv, 1 + b, partner)
        copy.start()
        i_copies.append(copy)

    l_target.wait()
    stores = []
    for b in range(2):
        i_copies[b].wait_recv()
        rows = pl.ds(b * HALF, HALF)
        resist = jax.nn.sigmoid(STEEP * (inten[b] + inten_got[b] - LEVEL))
        goal = target_v[rows, :].astype(F32)
        resist_v[rows, :] = resist
        weight[...] = 2.0 * (resist - goal) * STEEP * resist * (1.0 - resist)
        store = pltpu.make_async_copy(resist_v.at[rows], resist_h.at[rows], store_sem.at[b])
        store.start()
        stores.append(store)

        def back_columns(k, b=b):
            w = weight[...]
            load = jnp.concatenate([w * field[b, k, pl.ds(0, HALF), :], w * field[b, k, pl.ds(HALF, HALF), :]], axis=1)
            hi, lo = split(rows_by_table(load, block_of(place(inner, direct), place(inner, turned), 0)))
            c_stack[k, pl.ds(b * HALF, HALF), :] = hi
            c_stack[k, pl.ds(TILE + b * HALF, HALF), :] = lo

        loop(back_columns)

    f_copy.wait_send()
    f_part[...] = jnp.zeros((BAND, 2 * BAND), F32)

    def back_rows(k):
        hi, lo = c_stack[k, pl.ds(0, TILE), :], c_stack[k, pl.ds(TILE, TILE), :]
        value = table_by_rows([jnp.concatenate([freq_v[part, :BAND, :TILE], freq_v[part, :BAND, WINDOW : WINDOW + TILE]], axis=0) for part in range(2)], hi, lo)
        s_re = value[:BAND, :BAND] + value[BAND:, BAND:]
        s_im = value[:BAND, BAND:] - value[BAND:, :BAND]
        h_re, h_im = spec_v[0, k], spec_v[1, k]
        f_part[:, :BAND] += h_re * s_re + h_im * s_im
        f_part[:, BAND:] += h_re * s_im - h_im * s_re

    loop(back_rows)
    w_copy = remote(f_part, w_got, p_send, p_recv, 3, partner)
    w_copy.start()
    w_copy.wait_recv()

    lifted = rows_by_table((f_part[...] + w_got[...]) * (2.0 * SCALE), (freq_v[0], freq_v[1]))
    lifted = jnp.concatenate([lifted[:, :WINDOW], lifted[:, WINDOW:]], axis=0)
    hi, lo = split(lifted)
    edge_place = pl.ds(pl.multiple_of(TILE + kern * HALO, HALO), HALO)
    own_rows = place(pl.ds(half_at, HALF), direct)
    edge_grad = table_by_rows(place(edge_place, direct), hi, lo)
    side_grad = table_by_rows(own_rows, hi[:, TILE:], lo[:, TILE:])
    g_v[...] = edge_grad[:, :TILE]
    first, second = fold(side_grad[:64], side_grad[64:])
    g_side[0] = first
    g_side[1] = second
    first, second = fold(edge_grad[:32, TILE:], edge_grad[32:, TILE:])
    g_diag[0] = first
    g_diag[1] = second
    margin = exchange(g_v, g_side, g_diag, gg_v, gg_side, gg_diag, g_send, g_recv)
    each(margin, 0, lambda c: c.start())
    out_half[...] = table_by_rows(own_rows, hi[:, :TILE], lo[:, :TILE])
    each(margin, 1, lambda c: c.wait_recv())

    def added(x, lanes):
        mine = lax.broadcasted_iota(jnp.int32, lanes.shape, 1) < HALO
        zero = jnp.zeros(lanes.shape, F32)
        return x + jnp.concatenate([jnp.where(mine, lanes, zero), jnp.where(mine, zero, lanes)], axis=1)

    top, bottom = fold(gg_side[0], gg_side[1])
    out_half[...] = added(out_half[...], jnp.concatenate([top, bottom], axis=0))
    top, bottom = fold(gg_diag[0], gg_diag[1])
    near = pl.ds(pl.multiple_of(kern * HALO, HALO), HALO)
    out_half[near, :] = out_half[near, :] + added(gg_v[...], jnp.concatenate([top, bottom], axis=0))

    mine = grad_h.at[pl.ds(half_at, HALF)]
    g_copy = remote(out_half, mine, p_send, p_recv, 4, partner)
    g_copy.start()
    store = pltpu.make_async_copy(out_half, mine, store_sem.at[2])
    store.start()
    stores.append(store)

    each(halo, 0, lambda c: c.wait_send())
    each(margin, 0, lambda c: c.wait_send())
    for copy in i_copies:
        copy.wait_send()
    w_copy.wait_send()
    for store in stores:
        store.wait()
    g_copy.wait()


def on_device(mask, target, spectra):
    tables = make_tables()
    kernels = spectra.shape[1]
    vmem = lambda shape, dtype=F32: pltpu.VMEM(shape, dtype)
    dma = lambda n: pltpu.SemaphoreType.DMA((n,))
    scratch = [
        vmem((TILE, TILE)), vmem((TILE, TILE), jnp.int32), vmem(spectra.shape),
        *[vmem(t.shape, BF16) for t in tables],
        vmem((2, 64, 128)), vmem((2, 32, 128)),
        vmem((HALO, TILE)), vmem((2, 64, 128)), vmem((2, 32, 128)),
        vmem((HALF, TILE)), vmem((2, TILE, TILE), BF16),
        vmem((BAND, 2 * BAND)), vmem((BAND, 2 * BAND)),
        vmem((kernels, 2 * TILE, TILE), BF16), vmem((2, kernels, TILE, TILE)),
        vmem((2, HALF, TILE)), vmem((2, HALF, TILE)), vmem((HALF, TILE)), vmem((TILE, TILE)),
        vmem((kernels, 2 * TILE, TILE), BF16), vmem((BAND, 2 * BAND)), vmem((BAND, 2 * BAND)),
        vmem((HALO, TILE)), vmem((2, 64, 128)), vmem((2, 32, 128)),
        vmem((HALO, TILE)), vmem((2, 64, 128)), vmem((2, 32, 128)),
        vmem((HALF, TILE)),
        dma(5), dma(3), dma(5), dma(5), dma(5), dma(5), dma(5), dma(5),
    ]
    anywhere = pl.BlockSpec(memory_space=pl.ANY)
    outs = pl.pallas_call(
        body,
        out_shape=[jax.ShapeDtypeStruct((TILE, TILE), F32)] * 2,
        in_specs=[anywhere] * (3 + len(tables)),
        out_specs=[anywhere] * 2,
        scratch_shapes=scratch,
        compiler_params=pltpu.CompilerParams(
            collective_id=0, has_side_effects=True, vmem_limit_bytes=25165824
        ),
        name="socs_step",
    )(*[pltpu.with_memory_space_constraint(x, pltpu.HBM) for x in (mask, target, spectra, *map(jnp.asarray, tables))])

    def put(a, b, c, d):
        c[...] = a[...]
        d[...] = b[...]

    return pl.pallas_call(put, out_shape=[jax.ShapeDtypeStruct((TILE, TILE), F32)] * 2, name="put", compiler_params=pltpu.CompilerParams(vmem_limit_bytes=4 * 1024 * 1024))(*outs)


def solution(mesh):
    return jax.shard_map(
        on_device,
        mesh=mesh,
        in_specs=(P("ty", "tx"), P("ty", "tx"), P(None, "kern", None, None)),
        out_specs=(P("ty", "tx"), P("ty", "tx")),
        check_vma=False,
    )
```

```python
import math

import jax
import jax.numpy as jnp
import numpy as np
from jax import lax
from jax.experimental import pallas as pl
from jax.experimental.pallas import tpu as pltpu
from jax.sharding import PartitionSpec as P

TILE = 256
HALO = 64
BAND = 128
WINDOW = TILE + 2 * HALO
HALF = TILE // 2
STEEP = 8.0
LEVEL = 1.0
SCALE = 1.0 / (WINDOW * WINDOW)
MESH = pl.DeviceIdType.MESH
F32 = jnp.float32
BF16 = jnp.bfloat16


def halves(table):
    table = np.asarray(table, np.float32)
    hi = table.astype(BF16)
    lo = (table - hi.astype(np.float32)).astype(BF16)
    return hi, lo


def make_tables():
    freq = np.arange(BAND) - BAND // 2
    order = np.concatenate(
        [np.arange(TILE) + HALO, np.arange(HALO), np.arange(HALO) + HALO + TILE]
    )

    def waves(places):
        angle = np.mod(places[:, None] * freq[None, :], 2 * WINDOW) * (math.pi / WINDOW)
        return np.cos(angle), np.sin(angle)

    c, s = waves(2 * order - (WINDOW - 1))
    by_place = np.concatenate([c, -s], 1)
    by_freq = np.block([[c.T, s.T], [-s.T, c.T]])
    c, s = waves(2 * np.arange(HALF) + 1)
    fold_place = np.concatenate([c, s], 1)
    fold_freq = np.concatenate([c.T, s.T], 1)
    return [np.stack(halves(t)) for t in (by_place, by_freq, fold_place, fold_freq)]


def split(x):
    hi = x.astype(BF16)
    return hi, (x - hi.astype(F32)).astype(BF16)


def dot(a, b):
    return jnp.dot(a, b, preferred_element_type=F32)


def rows_by_table(x, table):
    hi, lo = split(x)
    t_hi, t_lo = table
    left = jnp.concatenate([hi, lo, hi], axis=1)
    return dot(left, jnp.concatenate([t_hi, t_hi, t_lo], axis=0))


def table_by_rows(table, hi, lo):
    t_hi, t_lo = table
    left = jnp.concatenate([t_hi, t_hi, t_lo], axis=1)
    return dot(left, jnp.concatenate([hi, lo, hi], axis=0))


def place_of(order, blocks):
    size = TILE // (2 * blocks)
    block, inside = order // (2 * size), order % (2 * size)
    return jnp.where(inside < size, HALF + block * size + inside, HALF - 1 - block * size - (inside - size))


def reorder(blocks, to_folded):
    rows = lax.broadcasted_iota(jnp.int32, (TILE, TILE), 0)
    lanes = lax.broadcasted_iota(jnp.int32, (TILE, TILE), 1)
    hit = (place_of(rows, blocks) == lanes) if to_folded else (rows == place_of(lanes, blocks))
    return hit.astype(F32).astype(BF16)


def fold(a, b):
    left_lanes = lax.broadcasted_iota(jnp.int32, a.shape, 1) < HALO
    first = jnp.where(left_lanes, a, pltpu.roll(b, HALO, 1))
    second = jnp.where(left_lanes, pltpu.roll(a, HALO, 1), b)
    return first, second


def body(
    mask_h, target_h, spec_h, place_h, freq_h, fplace_h, ffreq_h,
    resist_h, grad_h,
    mask_v, target_v, spec_v, place_v, freq_v, fplace_v, ffreq_v,
    send_side, send_diag, got_v, got_side, got_diag,
    acc_half, a_stack, f_part, f_got, r_stack, field, inten, inten_got, weight, goal, resist_p, resist_v,
    c_stack, w_part, w_got, g_v, g_side, g_diag, gg_v, gg_side, gg_diag, out_half,
    load_sem, store_sem, h_send, h_recv, p_send, p_recv, g_send, g_recv,
):
    kern, ty, tx = lax.axis_index("kern"), lax.axis_index("ty"), lax.axis_index("tx")
    n_ty, n_tx = lax.axis_size("ty"), lax.axis_size("tx")
    other = 1 - kern
    vt = ty - 1 + 2 * kern
    has_v = jnp.logical_and(vt >= 0, vt < n_ty)
    has_l, has_r = tx > 0, tx < n_tx - 1
    has_dl, has_dr = jnp.logical_and(has_v, has_l), jnp.logical_and(has_v, has_r)
    partner = (other, ty, tx)
    vertical = (other, vt, tx)
    left, right = (kern, ty, tx - 1), (kern, ty, tx + 1)
    diag_l, diag_r = (other, vt, tx - 1), (other, vt, tx + 1)
    peers = [(has_v, vertical), (has_l, left), (has_r, right), (has_dl, diag_l), (has_dr, diag_r)]

    barrier = pltpu.get_barrier_semaphore()
    pl.semaphore_signal(barrier, inc=1, device_id=partner, device_id_type=MESH)
    for has, peer in peers:

        @pl.when(has)
        def _(peer=peer):
            pl.semaphore_signal(barrier, inc=1, device_id=peer, device_id_type=MESH)

    loads = [
        (mask_h, mask_v), (place_h, place_v), (freq_h, freq_v), (spec_h, spec_v), (ffreq_h, ffreq_v),
        (fplace_h, fplace_v), (target_h, target_v),
    ]
    loads = [pltpu.make_async_copy(a, b, load_sem.at[i]) for i, (a, b) in enumerate(loads)]
    for load in loads:
        load.start()
    l_mask, l_place, l_freq, l_spec, l_ffreq, l_fplace, l_target = loads

    def place(rows, lanes):
        return place_v[0, rows, lanes], place_v[1, rows, lanes]

    def block_of(first, second, axis):
        return tuple(jnp.concatenate([a, b], axis=axis) for a, b in zip(first, second))

    inner, direct = slice(0, TILE), slice(0, 2 * BAND)
    edges = slice(TILE, WINDOW)

    a_stack[...] = jnp.zeros(a_stack.shape, BF16)
    for has, bufs in (
        (has_v, (got_v, gg_v)),
        (has_l, (got_side.at[0], gg_side.at[0])),
        (has_r, (got_side.at[1], gg_side.at[1])),
        (has_dl, (got_diag.at[0], gg_diag.at[0])),
        (has_dr, (got_diag.at[1], gg_diag.at[1])),
    ):

        @pl.when(jnp.logical_not(has))
        def _(bufs=bufs):
            for buf in bufs:
                buf[...] = jnp.zeros(buf.shape, F32)

    half_at = pl.multiple_of(kern * HALF, HALF)
    edge_at = pl.multiple_of(kern * (TILE - HALO), HALO)
    l_mask.wait()
    mask_half = mask_v[pl.ds(half_at, HALF), :]
    mask_edge = mask_v[pl.ds(edge_at, HALO), :]

    def side_lanes(x):
        lanes = lax.broadcasted_iota(jnp.int32, (x.shape[0], 128), 1) < HALO
        return jnp.where(lanes, x[:, :128], x[:, 128:])

    corners = side_lanes(mask_edge)
    first, second = fold(corners[:32], corners[32:])
    send_diag[0] = first
    send_diag[1] = second
    sides = side_lanes(mask_half)
    first, second = fold(sides[:64], sides[64:])
    send_side[0] = first
    send_side[1] = second

    pl.semaphore_wait(barrier, 1 + sum(has.astype(jnp.int32) for has, _ in peers))

    def remote(src, dst, send, recv, at, peer):
        return pltpu.make_async_remote_copy(
            src_ref=src, dst_ref=dst, send_sem=send.at[at], recv_sem=recv.at[at],
            device_id=peer, device_id_type=MESH,
        )

    def exchange(src_v, src_side, src_diag, dst_v, dst_side, dst_diag, send, recv):
        return (
            [
                (has_dl, has_dr, remote(src_diag.at[0], dst_diag.at[1], send, recv, 3, diag_l)),
                (has_dr, has_dl, remote(src_diag.at[1], dst_diag.at[0], send, recv, 4, diag_r)),
            ],
            [(has_v, has_v, remote(src_v, dst_v, send, recv, 0, vertical))],
            [
                (has_l, has_r, remote(src_side.at[0], dst_side.at[1], send, recv, 1, left)),
                (has_r, has_l, remote(src_side.at[1], dst_side.at[0], send, recv, 2, right)),
            ],
        )

    def each(copies, which, act):
        for entry in copies:

            @pl.when(entry[which])
            def _(copy=entry[2]):
                act(copy)

    h_diag, h_vert, h_side = exchange(
        mask_h.at[pl.ds(edge_at, HALO)], send_side, send_diag, got_v, got_side, got_diag,
        h_send, h_recv,
    )
    start = lambda c: c.start()
    arrived = lambda c: c.wait_recv()
    each(h_diag + h_vert + h_side, 0, start)

    l_place.wait()
    own = place(inner, direct)
    acc_half[...] = rows_by_table(mask_half, own)
    l_freq.wait()
    each(h_side, 1, arrived)
    top, bottom = fold(got_side[0], got_side[1])
    side_part = rows_by_table(jnp.concatenate([top, bottom], axis=0), place(edges, direct))
    half_hi, half_lo = split(acc_half[...] + side_part)
    a_stack[0, pl.ds(0, HALF), :] = half_hi
    a_stack[1, pl.ds(0, HALF), :] = half_lo
    each(h_vert, 1, arrived)
    g_v[...] = rows_by_table(got_v[...], own)
    each(h_diag, 1, arrived)
    top, bottom = fold(got_diag[0], got_diag[1])
    strip = g_v[...] + rows_by_table(jnp.concatenate([top, bottom], axis=0), place(edges, direct))
    edge_rows = pl.ds(pl.multiple_of(HALF + kern * HALO, HALO), HALO)
    for part, edge in enumerate(split(strip)):
        a_stack[part, edge_rows, :] = edge
    half_lanes = pl.ds(half_at, HALF)
    own_y = []
    for part in range(2):
        cos = [freq_v[part, pl.ds(0, BAND), half_lanes], freq_v[part, :BAND, TILE:WINDOW]]
        sin_lanes = pl.ds(pl.multiple_of(WINDOW + half_at, HALF), HALF)
        sin = [freq_v[part, pl.ds(0, BAND), sin_lanes], freq_v[part, :BAND, WINDOW + TILE :]]
        own_y.append(jnp.concatenate([jnp.concatenate(cos, axis=1), jnp.concatenate(sin, axis=1)], axis=0))
    full = table_by_rows(own_y, a_stack[0], a_stack[1])
    f_part[:, :BAND] = full[:BAND, :BAND] + full[BAND:, BAND:]
    f_part[:, BAND:] = full[:BAND, BAND:] - full[BAND:, :BAND]
    f_copy = remote(f_part, f_got, p_send, p_recv, 0, partner)
    f_copy.start()
    l_target.wait()
    folded = dot(reorder(2, True), target_v[...].astype(F32).astype(BF16))
    goal[...] = dot(folded.astype(BF16), reorder(1, False))
    l_spec.wait()
    l_ffreq.wait()
    l_fplace.wait()
    f_copy.wait_recv()
    w_part[...] = (f_part[...] + f_got[...]) * SCALE

    kernels = spec_v.shape[1]

    def loop(step):
        for k in range(kernels):
            step(k)

    def to_columns(k):
        f_re, f_im = w_part[:, :BAND], w_part[:, BAND:]
        h_re, h_im = spec_v[0, k], spec_v[1, k]
        prod = jnp.concatenate([f_re * h_re - f_im * h_im, f_re * h_im + f_im * h_re], axis=0)
        value = rows_by_table(prod, (ffreq_v[0], ffreq_v[1]))
        re_c, re_s, im_c, im_s = value[:BAND, :HALF], value[:BAND, HALF:], value[BAND:, :HALF], value[BAND:, HALF:]
        hi, lo = split(jnp.concatenate([re_c - im_s, re_c + im_s, im_c + re_s, im_c - re_s], axis=1))
        r_stack[k, pl.ds(0, BAND), :] = hi
        r_stack[k, pl.ds(BAND, BAND), :] = lo

    loop(to_columns)

    i_copies = []
    for b in range(2):
        inten[b] = jnp.zeros((HALF, TILE), F32)

        def to_rows(k, b=b):
            at = slice(b * 64, b * 64 + 64)
            hi, lo = r_stack[k, pl.ds(0, BAND), :], r_stack[k, pl.ds(BAND, BAND), :]
            table = [jnp.concatenate([fplace_v[p, at, :BAND], fplace_v[p, at, BAND:]], axis=0) for p in range(2)]
            value = table_by_rows(table, hi, lo)
            c_re, c_im, s_re, s_im = value[:64, :TILE], value[:64, TILE:], value[64:, :TILE], value[64:, TILE:]
            re = jnp.concatenate([c_re - s_im, c_re + s_im], axis=0)
            im = jnp.concatenate([c_im + s_re, c_im - s_re], axis=0)
            field[b, k, pl.ds(0, HALF), :] = re
            field[b, k, pl.ds(HALF, HALF), :] = im
            inten[b] += re * re + im * im

        loop(to_rows)
        copy = remote(inten.at[b], inten_got.at[b], p_send, p_recv, 1 + b, partner)
        copy.start()
        i_copies.append(copy)

    stores = []
    for b in range(2):
        i_copies[b].wait_recv()
        rows = pl.ds(b * HALF, HALF)
        resist = jax.nn.sigmoid(STEEP * (inten[b] + inten_got[b] - LEVEL))
        resist_p[rows, :] = resist
        weight[...] = 2.0 * (resist - goal[rows, :]) * STEEP * resist * (1.0 - resist)

        def back_columns(k, b=b):
            w = weight[...]
            re, im = w * field[b, k, pl.ds(0, HALF), :], w * field[b, k, pl.ds(HALF, HALF), :]
            even_re, odd_re = re[:, :HALF] + re[:, HALF:], re[:, HALF:] - re[:, :HALF]
            even_im, odd_im = im[:, :HALF] + im[:, HALF:], im[:, :HALF] - im[:, HALF:]
            hi, lo = split(
                jnp.concatenate(
                    [jnp.concatenate([even_re, odd_im], axis=1), jnp.concatenate([even_im, odd_re], axis=1)], axis=0
                )
            )
            cos = jnp.concatenate([fplace_v[0, :, :BAND], fplace_v[1, :, :BAND]], axis=1)
            sin = jnp.concatenate([fplace_v[0, :, BAND:], fplace_v[1, :, BAND:]], axis=1)
            value = dot(jnp.concatenate([hi, lo], axis=1), jnp.concatenate([cos, sin, cos, sin], axis=0))
            value = value[:, :BAND] + value[:, BAND:]
            p_re, m_re, p_im, m_im = value[:64], value[64:HALF], value[HALF : HALF + 64], value[HALF + 64 :]
            even = jnp.concatenate([p_re + m_re, p_im + m_im], axis=1)
            odd = jnp.concatenate([p_im - m_im, m_re - p_re], axis=1)
            for at, part in ((0, even), (HALF, odd)):
                hi, lo = split(part)
                c_stack[k, pl.ds(at + b * 64, 64), :] = hi
                c_stack[k, pl.ds(TILE + at + b * 64, 64), :] = lo

        loop(back_columns)

    f_copy.wait_send()
    f_part[...] = jnp.zeros((BAND, 2 * BAND), F32)

    def back_rows(k):
        hi, lo = c_stack[k, pl.ds(0, TILE), :], c_stack[k, pl.ds(TILE, TILE), :]
        value = table_by_rows((ffreq_v[0], ffreq_v[1]), hi, lo)
        s_re, s_im = value[:, :BAND], value[:, BAND:]
        h_re, h_im = spec_v[0, k], spec_v[1, k]
        f_part[:, :BAND] += h_re * s_re + h_im * s_im
        f_part[:, BAND:] += h_re * s_im - h_im * s_re

    loop(back_rows)
    w_copy = remote(f_part, w_got, p_send, p_recv, 3, partner)
    w_copy.start()
    high = resist_p[...].astype(BF16)
    rest = resist_p[...] - high.astype(F32)
    mid, low = split(rest)
    moved = dot(reorder(2, False), jnp.concatenate([high, mid, low], axis=1)).astype(BF16)
    lanes = reorder(1, True)
    resist_v[...] = dot(moved, jnp.concatenate([lanes, lanes, lanes], axis=0))
    store = pltpu.make_async_copy(resist_v, resist_h, store_sem.at[0])
    store.start()
    stores.append(store)
    w_copy.wait_recv()

    lifted = rows_by_table((f_part[...] + w_got[...]) * (2.0 * SCALE), (freq_v[0], freq_v[1]))
    lifted = jnp.concatenate([lifted[:, :WINDOW], lifted[:, WINDOW:]], axis=0)
    hi, lo = split(lifted)
    edge_place = pl.ds(pl.multiple_of(TILE + kern * HALO, HALO), HALO)
    own_rows = place(pl.ds(half_at, HALF), direct)
    edge_grad = table_by_rows(place(edge_place, direct), hi, lo)
    g_diag[...] = jnp.stack(fold(edge_grad[:32, TILE:], edge_grad[32:, TILE:]))
    g_v[...] = edge_grad[:, :TILE]
    m_diag, m_vert, m_side = exchange(g_v, g_side, g_diag, gg_v, gg_side, gg_diag, g_send, g_recv)
    each(m_diag + m_vert, 0, start)
    side_grad = table_by_rows(own_rows, hi[:, TILE:], lo[:, TILE:])
    g_side[...] = jnp.stack(fold(side_grad[:64], side_grad[64:]))
    each(m_side, 0, start)
    out_half[...] = table_by_rows(own_rows, hi[:, :TILE], lo[:, :TILE])
    each(m_side, 1, arrived)

    def added(x, lanes):
        mine = lax.broadcasted_iota(jnp.int32, lanes.shape, 1) < HALO
        zero = jnp.zeros(lanes.shape, F32)
        return x + jnp.concatenate([jnp.where(mine, lanes, zero), jnp.where(mine, zero, lanes)], axis=1)

    top, bottom = fold(gg_side[0], gg_side[1])
    out_half[...] = added(out_half[...], jnp.concatenate([top, bottom], axis=0))
    near = pl.ds(pl.multiple_of(kern * HALO, HALO), HALO)
    far = pl.ds(pl.multiple_of(other * HALO, HALO), HALO)
    near_h = pl.ds(pl.multiple_of(half_at + kern * HALO, HALO), HALO)
    far_h = pl.ds(pl.multiple_of(half_at + other * HALO, HALO), HALO)
    g_copies = []

    def give(at, at_h, n):
        g_copies.append(remote(out_half.at[at], grad_h.at[at_h], p_send, p_recv, n, partner))
        g_copies[-1].start()
        stores.append(pltpu.make_async_copy(out_half.at[at], grad_h.at[at_h], store_sem.at[n - 3]))
        stores[-1].start()

    give(far, far_h, 4)
    each(m_vert, 1, arrived)
    out_half[near, :] = out_half[near, :] + gg_v[...]
    each(m_diag, 1, arrived)
    top, bottom = fold(gg_diag[0], gg_diag[1])
    out_half[near, :] = added(out_half[near, :], jnp.concatenate([top, bottom], axis=0))
    give(near, near_h, 5)

    each(h_diag + h_vert + h_side + m_diag + m_vert + m_side, 0, lambda c: c.wait_send())
    for copy in i_copies:
        copy.wait_send()
    w_copy.wait_send()
    for store in stores:
        store.wait()
    for copy in g_copies:
        copy.wait()


def on_device(mask, target, spectra):
    tables = make_tables()
    kernels = spectra.shape[1]
    vmem = lambda shape, dtype=F32: pltpu.VMEM(shape, dtype)
    dma = lambda n: pltpu.SemaphoreType.DMA((n,))
    scratch = [
        vmem((TILE, TILE)), vmem((TILE, TILE), jnp.int32), vmem(spectra.shape),
        *[vmem(t.shape, BF16) for t in tables],
        vmem((2, 64, 128)), vmem((2, 32, 128)),
        vmem((HALO, TILE)), vmem((2, 64, 128)), vmem((2, 32, 128)),
        vmem((HALF, TILE)), vmem((2, TILE, TILE), BF16),
        vmem((BAND, 2 * BAND)), vmem((BAND, 2 * BAND)),
        vmem((kernels, 2 * BAND, 2 * TILE), BF16), vmem((2, kernels, TILE, TILE)),
        vmem((2, HALF, TILE)), vmem((2, HALF, TILE)), vmem((HALF, TILE)), vmem((TILE, TILE)), vmem((TILE, TILE)), vmem((TILE, TILE)),
        vmem((kernels, 2 * TILE, TILE), BF16), vmem((BAND, 2 * BAND)), vmem((BAND, 2 * BAND)),
        vmem((HALO, TILE)), vmem((2, 64, 128)), vmem((2, 32, 128)),
        vmem((HALO, TILE)), vmem((2, 64, 128)), vmem((2, 32, 128)),
        vmem((HALF, TILE)),
        dma(7), dma(3), dma(5), dma(5), dma(6), dma(6), dma(5), dma(5),
    ]
    anywhere = pl.BlockSpec(memory_space=pl.ANY)
    outs = pl.pallas_call(
        body,
        out_shape=[jax.ShapeDtypeStruct((TILE, TILE), F32)] * 2,
        in_specs=[anywhere] * (3 + len(tables)),
        out_specs=[anywhere] * 2,
        scratch_shapes=scratch,
        compiler_params=pltpu.CompilerParams(
            collective_id=0, has_side_effects=True, vmem_limit_bytes=25165824
        ),
        name="socs_step",
    )(*[pltpu.with_memory_space_constraint(x, pltpu.HBM) for x in (mask, target, spectra, *map(jnp.asarray, tables))])

    def put(a, b, c, d):
        c[...] = a[...]
        d[...] = b[...]

    return pl.pallas_call(put, out_shape=[jax.ShapeDtypeStruct((TILE, TILE), F32)] * 2, name="put", compiler_params=pltpu.CompilerParams(vmem_limit_bytes=4 * 1024 * 1024))(*outs)


def solution(mesh):
    return jax.shard_map(
        on_device,
        mesh=mesh,
        in_specs=(P("ty", "tx"), P("ty", "tx"), P(None, "kern", None, None)),
        out_specs=(P("ty", "tx"), P("ty", "tx")),
        check_vma=False,
    )
```

```python
import math

import jax
import jax.numpy as jnp
import numpy as np
from jax import lax
from jax.experimental import pallas as pl
from jax.experimental.pallas import tpu as pltpu
from jax.sharding import PartitionSpec as P

TILE = 256
HALO = 64
BAND = 128
WINDOW = TILE + 2 * HALO
HALF = TILE // 2
STEEP = 8.0
LEVEL = 1.0
SCALE = 1.0 / (WINDOW * WINDOW)
MESH = pl.DeviceIdType.MESH
F32 = jnp.float32
BF16 = jnp.bfloat16


def halves(table):
    table = np.asarray(table, np.float32)
    hi = table.astype(BF16)
    lo = (table - hi.astype(np.float32)).astype(BF16)
    return hi, lo


def make_tables():
    freq = np.arange(BAND) - BAND // 2
    order = np.concatenate(
        [np.arange(TILE) + HALO, np.arange(HALO), np.arange(HALO) + HALO + TILE]
    )

    def waves(places):
        angle = np.mod(places[:, None] * freq[None, :], 2 * WINDOW) * (math.pi / WINDOW)
        return np.cos(angle), np.sin(angle)

    c, s = waves(2 * order - (WINDOW - 1))
    by_place = np.concatenate([c, -s], 1)
    by_freq = np.block([[c.T, s.T], [-s.T, c.T]])
    c, s = waves(2 * np.arange(HALF) + 1)
    fold_place = np.concatenate([c, s], 1)
    fold_freq = np.concatenate([c.T, s.T], 1)
    return [np.stack(halves(t)) for t in (by_place, by_freq, fold_place, fold_freq)]


def split(x):
    hi = x.astype(BF16)
    return hi, (x - hi.astype(F32)).astype(BF16)


def dot(a, b):
    return jnp.dot(a, b, preferred_element_type=F32)


def rows_by_table(x, table):
    hi, lo = split(x)
    t_hi, t_lo = table
    left = jnp.concatenate([hi, lo, hi], axis=1)
    return dot(left, jnp.concatenate([t_hi, t_hi, t_lo], axis=0))


def table_by_rows(table, hi, lo):
    t_hi, t_lo = table
    left = jnp.concatenate([t_hi, t_hi, t_lo], axis=1)
    return dot(left, jnp.concatenate([hi, lo, hi], axis=0))


def place_of(order, blocks):
    size = TILE // (2 * blocks)
    block, inside = order // (2 * size), order % (2 * size)
    return jnp.where(inside < size, HALF + block * size + inside, HALF - 1 - block * size - (inside - size))


def reorder(blocks, to_folded):
    rows = lax.broadcasted_iota(jnp.int32, (TILE, TILE), 0)
    lanes = lax.broadcasted_iota(jnp.int32, (TILE, TILE), 1)
    hit = (place_of(rows, blocks) == lanes) if to_folded else (rows == place_of(lanes, blocks))
    return hit.astype(F32).astype(BF16)


def fold(a, b):
    left_lanes = lax.broadcasted_iota(jnp.int32, a.shape, 1) < HALO
    first = jnp.where(left_lanes, a, pltpu.roll(b, HALO, 1))
    second = jnp.where(left_lanes, pltpu.roll(a, HALO, 1), b)
    return first, second


def body(
    mask_h, target_h, spec_h, place_h, freq_h, fplace_h, ffreq_h,
    resist_h, grad_h,
    mask_v, target_v, spec_v, place_v, freq_v, fplace_v, ffreq_v,
    send_side, send_diag, got_v, got_side, got_diag,
    acc_half, a_stack, f_part, f_got, r_stack, field, inten, inten_got, weight, goal, resist_p, resist_v,
    c_stack, w_part, w_got, g_v, g_side, g_diag, gg_v, gg_side, gg_diag, out_half,
    load_sem, store_sem, h_send, h_recv, p_send, p_recv, g_send, g_recv,
):
    kern, ty, tx = lax.axis_index("kern"), lax.axis_index("ty"), lax.axis_index("tx")
    n_ty, n_tx = lax.axis_size("ty"), lax.axis_size("tx")
    other = 1 - kern
    vt = ty - 1 + 2 * kern
    has_v = jnp.logical_and(vt >= 0, vt < n_ty)
    has_l, has_r = tx > 0, tx < n_tx - 1
    has_dl, has_dr = jnp.logical_and(has_v, has_l), jnp.logical_and(has_v, has_r)
    partner = (other, ty, tx)
    vertical = (other, vt, tx)
    left, right = (kern, ty, tx - 1), (kern, ty, tx + 1)
    diag_l, diag_r = (other, vt, tx - 1), (other, vt, tx + 1)
    peers = [(has_v, vertical), (has_l, left), (has_r, right), (has_dl, diag_l), (has_dr, diag_r)]

    loads = [
        (mask_h, mask_v), (place_h, place_v), (freq_h, freq_v), (spec_h, spec_v), (ffreq_h, ffreq_v),
        (fplace_h, fplace_v), (target_h, target_v),
    ]
    loads = [pltpu.make_async_copy(a, b, load_sem.at[i]) for i, (a, b) in enumerate(loads)]
    loads[0].start()
    barrier = pltpu.get_barrier_semaphore()
    pl.semaphore_signal(barrier, inc=1, device_id=partner, device_id_type=MESH)
    for has, peer in peers:

        @pl.when(has)
        def _(peer=peer):
            pl.semaphore_signal(barrier, inc=1, device_id=peer, device_id_type=MESH)

    for load in loads[1:]:
        load.start()
    l_mask, l_place, l_freq, l_spec, l_ffreq, l_fplace, l_target = loads

    def place(rows, lanes):
        return place_v[0, rows, lanes], place_v[1, rows, lanes]

    inner, direct = slice(0, TILE), slice(0, 2 * BAND)
    edges = slice(TILE, WINDOW)

    half_at = pl.multiple_of(kern * HALF, HALF)
    edge_at = pl.multiple_of(kern * (TILE - HALO), HALO)
    l_mask.wait()
    mask_half = mask_v[pl.ds(half_at, HALF), :]
    mask_edge = mask_v[pl.ds(edge_at, HALO), :]

    def side_lanes(x):
        lanes = lax.broadcasted_iota(jnp.int32, (x.shape[0], 128), 1) < HALO
        return jnp.where(lanes, x[:, :128], x[:, 128:])

    corners = side_lanes(mask_edge)
    first, second = fold(corners[:32], corners[32:])
    send_diag[0] = first
    send_diag[1] = second
    sides = side_lanes(mask_half)
    first, second = fold(sides[:64], sides[64:])
    send_side[0] = first
    send_side[1] = second

    pl.semaphore_wait(barrier, 1 + sum(has.astype(jnp.int32) for has, _ in peers))

    def remote(src, dst, send, recv, at, peer):
        return pltpu.make_async_remote_copy(
            src_ref=src, dst_ref=dst, send_sem=send.at[at], recv_sem=recv.at[at],
            device_id=peer, device_id_type=MESH,
        )

    def exchange(src_v, src_side, src_diag, dst_v, dst_side, dst_diag, send, recv):
        return (
            [
                (has_dl, has_dr, remote(src_diag.at[0], dst_diag.at[1], send, recv, 3, diag_l)),
                (has_dr, has_dl, remote(src_diag.at[1], dst_diag.at[0], send, recv, 4, diag_r)),
            ],
            [(has_v, has_v, remote(src_v, dst_v, send, recv, 0, vertical))],
            [
                (has_l, has_r, remote(src_side.at[0], dst_side.at[1], send, recv, 1, left)),
                (has_r, has_l, remote(src_side.at[1], dst_side.at[0], send, recv, 2, right)),
            ],
        )

    def each(copies, which, act):
        for entry in copies:

            @pl.when(entry[which])
            def _(copy=entry[2]):
                act(copy)

    h_diag, h_vert, h_side = exchange(
        mask_h.at[pl.ds(edge_at, HALO)], send_side, send_diag, got_v, got_side, got_diag,
        h_send, h_recv,
    )
    start = lambda c: c.start()
    arrived = lambda c: c.wait_recv()
    each(h_diag + h_vert + h_side, 0, start)

    a_stack[...] = jnp.zeros(a_stack.shape, BF16)
    for has, bufs in (
        (has_v, (got_v, gg_v)),
        (has_l, (got_side.at[0], gg_side.at[0])),
        (has_r, (got_side.at[1], gg_side.at[1])),
        (has_dl, (got_diag.at[0], gg_diag.at[0])),
        (has_dr, (got_diag.at[1], gg_diag.at[1])),
    ):

        @pl.when(jnp.logical_not(has))
        def _(bufs=bufs):
            for buf in bufs:
                buf[...] = jnp.zeros(buf.shape, F32)


    l_place.wait()
    own = place(inner, direct)
    acc_half[...] = rows_by_table(mask_half, own)
    l_freq.wait()
    each(h_side, 1, arrived)
    top, bottom = fold(got_side[0], got_side[1])
    side_part = rows_by_table(jnp.concatenate([top, bottom], axis=0), place(edges, direct))
    half_hi, half_lo = split(acc_half[...] + side_part)
    a_stack[0, pl.ds(0, HALF), :] = half_hi
    a_stack[1, pl.ds(0, HALF), :] = half_lo
    each(h_vert, 1, arrived)
    g_v[...] = rows_by_table(got_v[...], own)
    each(h_diag, 1, arrived)
    top, bottom = fold(got_diag[0], got_diag[1])
    strip = g_v[...] + rows_by_table(jnp.concatenate([top, bottom], axis=0), place(edges, direct))
    edge_rows = pl.ds(pl.multiple_of(HALF + kern * HALO, HALO), HALO)
    for part, edge in enumerate(split(strip)):
        a_stack[part, edge_rows, :] = edge
    half_lanes = pl.ds(half_at, HALF)
    own_y = []
    for part in range(2):
        cos = [freq_v[part, pl.ds(0, BAND), half_lanes], freq_v[part, :BAND, TILE:WINDOW]]
        sin_lanes = pl.ds(pl.multiple_of(WINDOW + half_at, HALF), HALF)
        sin = [freq_v[part, pl.ds(0, BAND), sin_lanes], freq_v[part, :BAND, WINDOW + TILE :]]
        own_y.append(jnp.concatenate([jnp.concatenate(cos, axis=1), jnp.concatenate(sin, axis=1)], axis=0))
    full = table_by_rows(own_y, a_stack[0], a_stack[1])
    f_part[:, :BAND] = full[:BAND, :BAND] + full[BAND:, BAND:]
    f_part[:, BAND:] = full[:BAND, BAND:] - full[BAND:, :BAND]
    f_copy = remote(f_part, f_got, p_send, p_recv, 0, partner)
    f_copy.start()
    l_target.wait()
    folded = dot(reorder(2, True), target_v[...].astype(F32).astype(BF16))
    goal[...] = dot(folded.astype(BF16), reorder(1, False))
    l_spec.wait()
    l_ffreq.wait()
    l_fplace.wait()
    f_copy.wait_recv()
    w_part[...] = (f_part[...] + f_got[...]) * SCALE

    kernels = spec_v.shape[1]

    def loop(step):
        for k in range(kernels):
            step(k)

    def to_columns(k):
        f_re, f_im = w_part[:, :BAND], w_part[:, BAND:]
        h_re, h_im = spec_v[0, k], spec_v[1, k]
        prod = jnp.concatenate([f_re * h_re - f_im * h_im, f_re * h_im + f_im * h_re], axis=0)
        value = rows_by_table(prod, (ffreq_v[0], ffreq_v[1]))
        re_c, re_s, im_c, im_s = value[:BAND, :HALF], value[:BAND, HALF:], value[BAND:, :HALF], value[BAND:, HALF:]
        hi, lo = split(jnp.concatenate([re_c - im_s, re_c + im_s, im_c + re_s, im_c - re_s], axis=1))
        r_stack[k, pl.ds(0, BAND), :] = hi
        r_stack[k, pl.ds(BAND, BAND), :] = lo

    loop(to_columns)

    i_copies = []
    for b in range(2):
        inten[b] = jnp.zeros((HALF, TILE), F32)

        def to_rows(k, b=b):
            at = slice(b * 64, b * 64 + 64)
            hi, lo = r_stack[k, pl.ds(0, BAND), :], r_stack[k, pl.ds(BAND, BAND), :]
            table = [jnp.concatenate([fplace_v[p, at, :BAND], fplace_v[p, at, BAND:]], axis=0) for p in range(2)]
            value = table_by_rows(table, hi, lo)
            c_re, c_im, s_re, s_im = value[:64, :TILE], value[:64, TILE:], value[64:, :TILE], value[64:, TILE:]
            re = jnp.concatenate([c_re - s_im, c_re + s_im], axis=0)
            im = jnp.concatenate([c_im + s_re, c_im - s_re], axis=0)
            field[b, k, pl.ds(0, HALF), :] = re
            field[b, k, pl.ds(HALF, HALF), :] = im
            inten[b] += re * re + im * im

        loop(to_rows)
        copy = remote(inten.at[b], inten_got.at[b], p_send, p_recv, 1 + b, partner)
        copy.start()
        i_copies.append(copy)

    stores = []
    for b in range(2):
        i_copies[b].wait_recv()
        rows = pl.ds(b * HALF, HALF)
        resist = jax.nn.sigmoid(STEEP * (inten[b] + inten_got[b] - LEVEL))
        resist_p[rows, :] = resist
        weight[...] = 2.0 * (resist - goal[rows, :]) * STEEP * resist * (1.0 - resist)

        def back_columns(k, b=b):
            w = weight[...]
            re, im = w * field[b, k, pl.ds(0, HALF), :], w * field[b, k, pl.ds(HALF, HALF), :]
            even_re, odd_re = re[:, :HALF] + re[:, HALF:], re[:, HALF:] - re[:, :HALF]
            even_im, odd_im = im[:, :HALF] + im[:, HALF:], im[:, :HALF] - im[:, HALF:]
            hi, lo = split(
                jnp.concatenate(
                    [jnp.concatenate([even_re, odd_im], axis=1), jnp.concatenate([even_im, odd_re], axis=1)], axis=0
                )
            )
            cos = jnp.concatenate([fplace_v[0, :, :BAND], fplace_v[1, :, :BAND]], axis=1)
            sin = jnp.concatenate([fplace_v[0, :, BAND:], fplace_v[1, :, BAND:]], axis=1)
            value = dot(jnp.concatenate([hi, lo], axis=1), jnp.concatenate([cos, sin, cos, sin], axis=0))
            value = value[:, :BAND] + value[:, BAND:]
            p_re, m_re, p_im, m_im = value[:64], value[64:HALF], value[HALF : HALF + 64], value[HALF + 64 :]
            even = jnp.concatenate([p_re + m_re, p_im + m_im], axis=1)
            odd = jnp.concatenate([p_im - m_im, m_re - p_re], axis=1)
            for at, part in ((0, even), (HALF, odd)):
                hi, lo = split(part)
                c_stack[k, pl.ds(at + b * 64, 64), :] = hi
                c_stack[k, pl.ds(TILE + at + b * 64, 64), :] = lo

        loop(back_columns)

    f_copy.wait_send()
    f_part[...] = jnp.zeros((BAND, 2 * BAND), F32)

    def back_rows(k):
        hi, lo = c_stack[k, pl.ds(0, TILE), :], c_stack[k, pl.ds(TILE, TILE), :]
        value = table_by_rows((ffreq_v[0], ffreq_v[1]), hi, lo)
        s_re, s_im = value[:, :BAND], value[:, BAND:]
        h_re, h_im = spec_v[0, k], spec_v[1, k]
        f_part[:, :BAND] += h_re * s_re + h_im * s_im
        f_part[:, BAND:] += h_re * s_im - h_im * s_re

    loop(back_rows)
    w_copy = remote(f_part, w_got, p_send, p_recv, 3, partner)
    w_copy.start()
    high = resist_p[...].astype(BF16)
    rest = resist_p[...] - high.astype(F32)
    mid, low = split(rest)
    moved = dot(reorder(2, False), jnp.concatenate([high, mid, low], axis=1)).astype(BF16)
    lanes = reorder(1, True)
    resist_v[...] = dot(moved, jnp.concatenate([lanes, lanes, lanes], axis=0))
    store = pltpu.make_async_copy(resist_v, resist_h, store_sem.at[0])
    store.start()
    stores.append(store)
    w_copy.wait_recv()

    both = split((f_part[...] + w_got[...]) * (2.0 * SCALE))

    def lifted(rows):
        table = [jnp.concatenate([place_v[p, rows, :BAND], place_v[p, rows, BAND:]], axis=0) for p in range(2)]
        value = table_by_rows(table, *both)
        n = value.shape[0] // 2
        re = value[:n, :BAND] + value[n:, BAND:]
        return jnp.concatenate([re, value[:n, BAND:] - value[n:, :BAND]], axis=1)

    def spread(x, lanes):
        return rows_by_table(x, (freq_v[0, :, lanes], freq_v[1, :, lanes]))

    edge_grad = spread(lifted(pl.ds(pl.multiple_of(TILE + kern * HALO, HALO), HALO)), slice(0, WINDOW))
    g_diag[...] = jnp.stack(fold(edge_grad[:32, TILE:], edge_grad[32:, TILE:]))
    g_v[...] = edge_grad[:, :TILE]
    m_diag, m_vert, m_side = exchange(g_v, g_side, g_diag, gg_v, gg_side, gg_diag, g_send, g_recv)
    each(m_diag + m_vert, 0, start)
    half_lift = lifted(pl.ds(half_at, HALF))
    side_grad = spread(half_lift, slice(TILE, WINDOW))
    g_side[...] = jnp.stack(fold(side_grad[:64], side_grad[64:]))
    each(m_side, 0, start)
    out_half[...] = spread(half_lift, slice(0, TILE))
    each(m_side, 1, arrived)

    def added(x, lanes):
        mine = lax.broadcasted_iota(jnp.int32, lanes.shape, 1) < HALO
        zero = jnp.zeros(lanes.shape, F32)
        return x + jnp.concatenate([jnp.where(mine, lanes, zero), jnp.where(mine, zero, lanes)], axis=1)

    top, bottom = fold(gg_side[0], gg_side[1])
    out_half[...] = added(out_half[...], jnp.concatenate([top, bottom], axis=0))
    near = pl.ds(pl.multiple_of(kern * HALO, HALO), HALO)
    far = pl.ds(pl.multiple_of(other * HALO, HALO), HALO)
    near_h = pl.ds(pl.multiple_of(half_at + kern * HALO, HALO), HALO)
    far_h = pl.ds(pl.multiple_of(half_at + other * HALO, HALO), HALO)
    g_copies = []

    def give(at, at_h, n):
        g_copies.append(remote(out_half.at[at], grad_h.at[at_h], p_send, p_recv, n, partner))
        g_copies[-1].start()
        stores.append(pltpu.make_async_copy(out_half.at[at], grad_h.at[at_h], store_sem.at[n - 3]))
        stores[-1].start()

    give(far, far_h, 4)
    each(m_vert, 1, arrived)
    out_half[near, :] = out_half[near, :] + gg_v[...]
    each(m_diag, 1, arrived)
    top, bottom = fold(gg_diag[0], gg_diag[1])
    out_half[near, :] = added(out_half[near, :], jnp.concatenate([top, bottom], axis=0))
    give(near, near_h, 5)

    each(h_diag + h_vert + h_side + m_diag + m_vert + m_side, 0, lambda c: c.wait_send())
    for copy in i_copies:
        copy.wait_send()
    w_copy.wait_send()
    for store in stores:
        store.wait()
    for copy in g_copies:
        copy.wait()


def on_device(mask, target, spectra):
    tables = make_tables()
    kernels = spectra.shape[1]
    vmem = lambda shape, dtype=F32: pltpu.VMEM(shape, dtype)
    dma = lambda n: pltpu.SemaphoreType.DMA((n,))
    scratch = [
        vmem((TILE, TILE)), vmem((TILE, TILE), jnp.int32), vmem(spectra.shape),
        *[vmem(t.shape, BF16) for t in tables],
        vmem((2, 64, 128)), vmem((2, 32, 128)),
        vmem((HALO, TILE)), vmem((2, 64, 128)), vmem((2, 32, 128)),
        vmem((HALF, TILE)), vmem((2, TILE, TILE), BF16),
        vmem((BAND, 2 * BAND)), vmem((BAND, 2 * BAND)),
        vmem((kernels, 2 * BAND, 2 * TILE), BF16), vmem((2, kernels, TILE, TILE)),
        vmem((2, HALF, TILE)), vmem((2, HALF, TILE)), vmem((HALF, TILE)), vmem((TILE, TILE)), vmem((TILE, TILE)), vmem((TILE, TILE)),
        vmem((kernels, 2 * TILE, TILE), BF16), vmem((BAND, 2 * BAND)), vmem((BAND, 2 * BAND)),
        vmem((HALO, TILE)), vmem((2, 64, 128)), vmem((2, 32, 128)),
        vmem((HALO, TILE)), vmem((2, 64, 128)), vmem((2, 32, 128)),
        vmem((HALF, TILE)),
        dma(7), dma(3), dma(5), dma(5), dma(6), dma(6), dma(5), dma(5),
    ]
    anywhere = pl.BlockSpec(memory_space=pl.ANY)
    outs = pl.pallas_call(
        body,
        out_shape=[jax.ShapeDtypeStruct((TILE, TILE), F32)] * 2,
        in_specs=[anywhere] * (3 + len(tables)),
        out_specs=[anywhere] * 2,
        scratch_shapes=scratch,
        compiler_params=pltpu.CompilerParams(
            collective_id=0, has_side_effects=True, vmem_limit_bytes=25165824
        ),
        name="socs_step",
    )(*[pltpu.with_memory_space_constraint(x, pltpu.HBM) for x in (mask, target, spectra, *map(jnp.asarray, tables))])

    def put(a, b, c, d, sem):
        copies = [pltpu.make_async_copy(a, c, sem.at[0]), pltpu.make_async_copy(b, d, sem.at[1])]
        for copy in copies:
            copy.start()
        for copy in copies:
            copy.wait()

    return pl.pallas_call(put, out_shape=[jax.ShapeDtypeStruct((TILE, TILE), F32)] * 2, name="put", in_specs=[anywhere] * 2, out_specs=[anywhere] * 2, scratch_shapes=[dma(2)], compiler_params=pltpu.CompilerParams(vmem_limit_bytes=4 * 1024 * 1024))(*outs)


def solution(mesh):
    return jax.shard_map(
        on_device,
        mesh=mesh,
        in_specs=(P("ty", "tx"), P("ty", "tx"), P(None, "kern", None, None)),
        out_specs=(P("ty", "tx"), P("ty", "tx")),
        check_vma=False,
    )
```

```python
import math

import jax
import jax.numpy as jnp
import numpy as np
from jax import lax
from jax.experimental import pallas as pl
from jax.experimental.pallas import tpu as pltpu
from jax.sharding import PartitionSpec as P

TILE = 256
HALO = 64
BAND = 128
WINDOW = TILE + 2 * HALO
HALF = TILE // 2
STEEP = 8.0
LEVEL = 1.0
SCALE = 1.0 / (WINDOW * WINDOW)
MESH = pl.DeviceIdType.MESH
F32 = jnp.float32
BF16 = jnp.bfloat16


def halves(table):
    table = np.asarray(table, np.float32)
    hi = table.astype(BF16)
    lo = (table - hi.astype(np.float32)).astype(BF16)
    return hi, lo


def make_tables():
    freq = np.arange(BAND) - BAND // 2
    order = np.concatenate(
        [np.arange(TILE) + HALO, np.arange(HALO), np.arange(HALO) + HALO + TILE]
    )

    def waves(places):
        angle = np.mod(places[:, None] * freq[None, :], 2 * WINDOW) * (math.pi / WINDOW)
        return np.cos(angle), np.sin(angle)

    c, s = waves(2 * order - (WINDOW - 1))
    by_place = np.concatenate([c, -s], 1)
    by_freq = np.block([[c.T, s.T], [-s.T, c.T]])
    c, s = waves(2 * np.arange(HALF) + 1)
    fold_place = np.concatenate([c, s], 1)
    fold_freq = np.concatenate([c.T, s.T], 1)
    return [np.stack(halves(t)) for t in (by_place, by_freq, fold_place, fold_freq)]


def split(x):
    hi = x.astype(BF16)
    return hi, (x - hi.astype(F32)).astype(BF16)


def dot(a, b):
    return jnp.dot(a, b, preferred_element_type=F32)


def rows_by_table(x, table):
    hi, lo = split(x)
    t_hi, t_lo = table
    left = jnp.concatenate([hi, lo, hi], axis=1)
    return dot(left, jnp.concatenate([t_hi, t_hi, t_lo], axis=0))


def table_by_rows(table, hi, lo):
    t_hi, t_lo = table
    left = jnp.concatenate([t_hi, t_hi, t_lo], axis=1)
    return dot(left, jnp.concatenate([hi, lo, hi], axis=0))


def place_of(order, blocks):
    size = TILE // (2 * blocks)
    block, inside = order // (2 * size), order % (2 * size)
    return jnp.where(inside < size, HALF + block * size + inside, HALF - 1 - block * size - (inside - size))


def reorder(blocks, to_folded):
    rows = lax.broadcasted_iota(jnp.int32, (TILE, TILE), 0)
    lanes = lax.broadcasted_iota(jnp.int32, (TILE, TILE), 1)
    hit = (place_of(rows, blocks) == lanes) if to_folded else (rows == place_of(lanes, blocks))
    return hit.astype(F32).astype(BF16)


def fold(a, b):
    left_lanes = lax.broadcasted_iota(jnp.int32, a.shape, 1) < HALO
    first = jnp.where(left_lanes, a, pltpu.roll(b, HALO, 1))
    second = jnp.where(left_lanes, pltpu.roll(a, HALO, 1), b)
    return first, second


def body(
    mask_h, target_h, spec_h, place_h, freq_h, fplace_h, ffreq_h,
    resist_h, grad_h,
    mask_v, target_v, spec_v, place_v, freq_v, fplace_v, ffreq_v,
    send_side, send_diag, got_v, got_side, got_diag,
    acc_half, a_stack, f_part, f_got, r_stack, field, inten, inten_got, weight, goal, resist_p, resist_v,
    c_stack, w_part, w_got, g_v, g_side, g_diag, gg_v, gg_side, gg_diag, out_half,
    load_sem, store_sem, h_send, h_recv, p_send, p_recv, g_send, g_recv,
):
    kern, ty, tx = lax.axis_index("kern"), lax.axis_index("ty"), lax.axis_index("tx")
    n_ty, n_tx = lax.axis_size("ty"), lax.axis_size("tx")
    other = 1 - kern
    vt = ty - 1 + 2 * kern
    has_v = jnp.logical_and(vt >= 0, vt < n_ty)
    has_l, has_r = tx > 0, tx < n_tx - 1
    has_dl, has_dr = jnp.logical_and(has_v, has_l), jnp.logical_and(has_v, has_r)
    partner = (other, ty, tx)
    vertical = (other, vt, tx)
    left, right = (kern, ty, tx - 1), (kern, ty, tx + 1)
    diag_l, diag_r = (other, vt, tx - 1), (other, vt, tx + 1)
    peers = [(has_v, vertical), (has_l, left), (has_r, right), (has_dl, diag_l), (has_dr, diag_r)]

    loads = [
        (mask_h, mask_v), (place_h, place_v), (freq_h, freq_v), (spec_h, spec_v), (ffreq_h, ffreq_v),
        (fplace_h, fplace_v), (target_h, target_v),
    ]
    loads = [pltpu.make_async_copy(a, b, load_sem.at[i]) for i, (a, b) in enumerate(loads)]
    loads[0].start()
    barrier = pltpu.get_barrier_semaphore()
    pl.semaphore_signal(barrier, inc=1, device_id=partner, device_id_type=MESH)
    for has, peer in peers:

        @pl.when(has)
        def _(peer=peer):
            pl.semaphore_signal(barrier, inc=1, device_id=peer, device_id_type=MESH)

    for load in loads[1:]:
        load.start()
    l_mask, l_place, l_freq, l_spec, l_ffreq, l_fplace, l_target = loads

    def place(rows, lanes):
        return place_v[0, rows, lanes], place_v[1, rows, lanes]

    inner, direct = slice(0, TILE), slice(0, 2 * BAND)
    edges = slice(TILE, WINDOW)

    half_at = pl.multiple_of(kern * HALF, HALF)
    edge_at = pl.multiple_of(kern * (TILE - HALO), HALO)
    l_mask.wait()
    mask_half = mask_v[pl.ds(half_at, HALF), :]
    mask_edge = mask_v[pl.ds(edge_at, HALO), :]

    def side_lanes(x):
        lanes = lax.broadcasted_iota(jnp.int32, (x.shape[0], 128), 1) < HALO
        return jnp.where(lanes, x[:, :128], x[:, 128:])

    corners = side_lanes(mask_edge)
    first, second = fold(corners[:32], corners[32:])
    send_diag[0] = first
    send_diag[1] = second
    sides = side_lanes(mask_half)
    first, second = fold(sides[:64], sides[64:])
    send_side[0] = first
    send_side[1] = second

    pl.semaphore_wait(barrier, 1 + sum(has.astype(jnp.int32) for has, _ in peers))

    def remote(src, dst, send, recv, at, peer):
        return pltpu.make_async_remote_copy(
            src_ref=src, dst_ref=dst, send_sem=send.at[at], recv_sem=recv.at[at],
            device_id=peer, device_id_type=MESH,
        )

    def exchange(src_v, src_side, src_diag, dst_v, dst_side, dst_diag, send, recv):
        return (
            [
                (has_dl, has_dr, remote(src_diag.at[0], dst_diag.at[1], send, recv, 3, diag_l)),
                (has_dr, has_dl, remote(src_diag.at[1], dst_diag.at[0], send, recv, 4, diag_r)),
            ],
            [(has_v, has_v, remote(src_v, dst_v, send, recv, 0, vertical))],
            [
                (has_l, has_r, remote(src_side.at[0], dst_side.at[1], send, recv, 1, left)),
                (has_r, has_l, remote(src_side.at[1], dst_side.at[0], send, recv, 2, right)),
            ],
        )

    def each(copies, which, act):
        for entry in copies:

            @pl.when(entry[which])
            def _(copy=entry[2]):
                act(copy)

    h_diag, h_vert, h_side = exchange(
        mask_h.at[pl.ds(edge_at, HALO)], send_side, send_diag, got_v, got_side, got_diag,
        h_send, h_recv,
    )
    start = lambda c: c.start()
    arrived = lambda c: c.wait_recv()
    each(h_diag + h_vert + h_side, 0, start)

    a_stack[...] = jnp.zeros(a_stack.shape, BF16)
    for has, bufs in (
        (has_v, (got_v, gg_v)),
        (has_l, (got_side.at[0], gg_side.at[0])),
        (has_r, (got_side.at[1], gg_side.at[1])),
        (has_dl, (got_diag.at[0], gg_diag.at[0])),
        (has_dr, (got_diag.at[1], gg_diag.at[1])),
    ):

        @pl.when(jnp.logical_not(has))
        def _(bufs=bufs):
            for buf in bufs:
                buf[...] = jnp.zeros(buf.shape, F32)


    l_place.wait()
    own = place(inner, direct)
    acc_half[...] = rows_by_table(mask_half, own)
    l_freq.wait()
    each(h_side, 1, arrived)
    top, bottom = fold(got_side[0], got_side[1])
    side_part = rows_by_table(jnp.concatenate([top, bottom], axis=0), place(edges, direct))
    half_hi, half_lo = split(acc_half[...] + side_part)
    a_stack[0, pl.ds(0, HALF), :] = half_hi
    a_stack[1, pl.ds(0, HALF), :] = half_lo
    each(h_vert, 1, arrived)
    g_v[...] = rows_by_table(got_v[...], own)
    each(h_diag, 1, arrived)
    top, bottom = fold(got_diag[0], got_diag[1])
    strip = g_v[...] + rows_by_table(jnp.concatenate([top, bottom], axis=0), place(edges, direct))
    edge_rows = pl.ds(pl.multiple_of(HALF + kern * HALO, HALO), HALO)
    for part, edge in enumerate(split(strip)):
        a_stack[part, edge_rows, :] = edge
    half_lanes = pl.ds(half_at, HALF)
    own_y = []
    for part in range(2):
        cos = [freq_v[part, pl.ds(0, BAND), half_lanes], freq_v[part, :BAND, TILE:WINDOW]]
        sin_lanes = pl.ds(pl.multiple_of(WINDOW + half_at, HALF), HALF)
        sin = [freq_v[part, pl.ds(0, BAND), sin_lanes], freq_v[part, :BAND, WINDOW + TILE :]]
        own_y.append(jnp.concatenate([jnp.concatenate(cos, axis=1), jnp.concatenate(sin, axis=1)], axis=0))
    full = table_by_rows(own_y, a_stack[0], a_stack[1])
    f_part[:, :BAND] = full[:BAND, :BAND] + full[BAND:, BAND:]
    f_part[:, BAND:] = full[:BAND, BAND:] - full[BAND:, :BAND]
    f_copy = remote(f_part, f_got, p_send, p_recv, 0, partner)
    f_copy.start()
    l_target.wait()
    folded = dot(reorder(2, True), target_v[...].astype(F32).astype(BF16))
    goal[...] = dot(folded.astype(BF16), reorder(1, False))
    l_spec.wait()
    l_ffreq.wait()
    l_fplace.wait()
    f_copy.wait_recv()
    w_part[...] = (f_part[...] + f_got[...]) * SCALE

    kernels = spec_v.shape[1]

    def loop(step):
        for k in range(kernels):
            step(k)

    def to_columns(first):
        f_re, f_im = w_part[:, :BAND], w_part[:, BAND:]
        prods = []
        for k in (first, first + 1):
            h_re, h_im = spec_v[0, k], spec_v[1, k]
            prods += [f_re * h_re - f_im * h_im, f_re * h_im + f_im * h_re]
        both = rows_by_table(jnp.concatenate(prods, axis=0), (ffreq_v[0], ffreq_v[1]))
        for i in range(2):
            value = both[i * 2 * BAND : (i + 1) * 2 * BAND]
            re_c, re_s, im_c, im_s = value[:BAND, :HALF], value[:BAND, HALF:], value[BAND:, :HALF], value[BAND:, HALF:]
            hi, lo = split(jnp.concatenate([re_c - im_s, re_c + im_s, im_c + re_s, im_c - re_s], axis=1))
            r_stack[first + i, pl.ds(0, BAND), :] = hi
            r_stack[first + i, pl.ds(BAND, BAND), :] = lo

    for k in range(0, kernels, 2):
        to_columns(k)

    i_copies = []
    for b in range(2):
        inten[b] = jnp.zeros((HALF, TILE), F32)

        def to_rows(k, b=b):
            at = slice(b * 64, b * 64 + 64)
            hi, lo = r_stack[k, pl.ds(0, BAND), :], r_stack[k, pl.ds(BAND, BAND), :]
            table = [jnp.concatenate([fplace_v[p, at, :BAND], fplace_v[p, at, BAND:]], axis=0) for p in range(2)]
            value = table_by_rows(table, hi, lo)
            c_re, c_im, s_re, s_im = value[:64, :TILE], value[:64, TILE:], value[64:, :TILE], value[64:, TILE:]
            re = jnp.concatenate([c_re - s_im, c_re + s_im], axis=0)
            im = jnp.concatenate([c_im + s_re, c_im - s_re], axis=0)
            field[b, k, pl.ds(0, HALF), :] = re
            field[b, k, pl.ds(HALF, HALF), :] = im
            inten[b] += re * re + im * im

        loop(to_rows)
        copy = remote(inten.at[b], inten_got.at[b], p_send, p_recv, 1 + b, partner)
        copy.start()
        i_copies.append(copy)

    stores = []
    for b in range(2):
        i_copies[b].wait_recv()
        rows = pl.ds(b * HALF, HALF)
        resist = jax.nn.sigmoid(STEEP * (inten[b] + inten_got[b] - LEVEL))
        resist_p[rows, :] = resist
        weight[...] = 2.0 * (resist - goal[rows, :]) * STEEP * resist * (1.0 - resist)

        def back_columns(k, b=b):
            w = weight[...]
            re, im = w * field[b, k, pl.ds(0, HALF), :], w * field[b, k, pl.ds(HALF, HALF), :]
            even_re, odd_re = re[:, :HALF] + re[:, HALF:], re[:, HALF:] - re[:, :HALF]
            even_im, odd_im = im[:, :HALF] + im[:, HALF:], im[:, :HALF] - im[:, HALF:]
            hi, lo = split(
                jnp.concatenate(
                    [jnp.concatenate([even_re, odd_im], axis=1), jnp.concatenate([even_im, odd_re], axis=1)], axis=0
                )
            )
            cos = jnp.concatenate([fplace_v[0, :, :BAND], fplace_v[1, :, :BAND]], axis=1)
            sin = jnp.concatenate([fplace_v[0, :, BAND:], fplace_v[1, :, BAND:]], axis=1)
            value = dot(jnp.concatenate([hi, lo], axis=1), jnp.concatenate([cos, sin, cos, sin], axis=0))
            value = value[:, :BAND] + value[:, BAND:]
            p_re, m_re, p_im, m_im = value[:64], value[64:HALF], value[HALF : HALF + 64], value[HALF + 64 :]
            even = jnp.concatenate([p_re + m_re, p_im + m_im], axis=1)
            odd = jnp.concatenate([p_im - m_im, m_re - p_re], axis=1)
            for at, part in ((0, even), (HALF, odd)):
                hi, lo = split(part)
                c_stack[k, pl.ds(at + b * 64, 64), :] = hi
                c_stack[k, pl.ds(TILE + at + b * 64, 64), :] = lo

        loop(back_columns)

    f_copy.wait_send()
    f_part[...] = jnp.zeros((BAND, 2 * BAND), F32)

    def back_rows(k):
        hi, lo = c_stack[k, pl.ds(0, TILE), :], c_stack[k, pl.ds(TILE, TILE), :]
        value = table_by_rows((ffreq_v[0], ffreq_v[1]), hi, lo)
        s_re, s_im = value[:, :BAND], value[:, BAND:]
        h_re, h_im = spec_v[0, k], spec_v[1, k]
        f_part[:, :BAND] += h_re * s_re + h_im * s_im
        f_part[:, BAND:] += h_re * s_im - h_im * s_re

    loop(back_rows)
    w_copy = remote(f_part, w_got, p_send, p_recv, 3, partner)
    w_copy.start()
    high = resist_p[...].astype(BF16)
    rest = resist_p[...] - high.astype(F32)
    mid, low = split(rest)
    moved = dot(reorder(2, False), jnp.concatenate([high, mid, low], axis=1)).astype(BF16)
    lanes = reorder(1, True)
    resist_v[...] = dot(moved, jnp.concatenate([lanes, lanes, lanes], axis=0))
    store = pltpu.make_async_copy(resist_v, resist_h, store_sem.at[0])
    store.start()
    stores.append(store)
    w_copy.wait_recv()

    both = split((f_part[...] + w_got[...]) * (2.0 * SCALE))

    def lifted(rows):
        table = [jnp.concatenate([place_v[p, rows, :BAND], place_v[p, rows, BAND:]], axis=0) for p in range(2)]
        value = table_by_rows(table, *both)
        n = value.shape[0] // 2
        re = value[:n, :BAND] + value[n:, BAND:]
        return jnp.concatenate([re, value[:n, BAND:] - value[n:, :BAND]], axis=1)

    def spread(x, lanes):
        return rows_by_table(x, (freq_v[0, :, lanes], freq_v[1, :, lanes]))

    edge_grad = spread(lifted(pl.ds(pl.multiple_of(TILE + kern * HALO, HALO), HALO)), slice(0, WINDOW))
    g_diag[...] = jnp.stack(fold(edge_grad[:32, TILE:], edge_grad[32:, TILE:]))
    g_v[...] = edge_grad[:, :TILE]
    m_diag, m_vert, m_side = exchange(g_v, g_side, g_diag, gg_v, gg_side, gg_diag, g_send, g_recv)
    each(m_diag + m_vert, 0, start)
    half_lift = lifted(pl.ds(half_at, HALF))
    side_grad = spread(half_lift, slice(TILE, WINDOW))
    g_side[...] = jnp.stack(fold(side_grad[:64], side_grad[64:]))
    each(m_side, 0, start)
    out_half[...] = spread(half_lift, slice(0, TILE))
    each(m_side, 1, arrived)

    def added(x, lanes):
        mine = lax.broadcasted_iota(jnp.int32, lanes.shape, 1) < HALO
        zero = jnp.zeros(lanes.shape, F32)
        return x + jnp.concatenate([jnp.where(mine, lanes, zero), jnp.where(mine, zero, lanes)], axis=1)

    top, bottom = fold(gg_side[0], gg_side[1])
    out_half[...] = added(out_half[...], jnp.concatenate([top, bottom], axis=0))
    near = pl.ds(pl.multiple_of(kern * HALO, HALO), HALO)
    far = pl.ds(pl.multiple_of(other * HALO, HALO), HALO)
    near_h = pl.ds(pl.multiple_of(half_at + kern * HALO, HALO), HALO)
    far_h = pl.ds(pl.multiple_of(half_at + other * HALO, HALO), HALO)
    g_copies = []

    def give(at, at_h, n):
        g_copies.append(remote(out_half.at[at], grad_h.at[at_h], p_send, p_recv, n, partner))
        g_copies[-1].start()
        stores.append(pltpu.make_async_copy(out_half.at[at], grad_h.at[at_h], store_sem.at[n - 3]))
        stores[-1].start()

    give(far, far_h, 4)
    each(m_vert, 1, arrived)
    out_half[near, :] = out_half[near, :] + gg_v[...]
    each(m_diag, 1, arrived)
    top, bottom = fold(gg_diag[0], gg_diag[1])
    out_half[near, :] = added(out_half[near, :], jnp.concatenate([top, bottom], axis=0))
    give(near, near_h, 5)

    each(h_diag + h_vert + h_side + m_diag + m_vert + m_side, 0, lambda c: c.wait_send())
    for copy in i_copies:
        copy.wait_send()
    w_copy.wait_send()
    for store in stores:
        store.wait()
    for copy in g_copies:
        copy.wait()


def on_device(mask, target, spectra):
    tables = make_tables()
    kernels = spectra.shape[1]
    vmem = lambda shape, dtype=F32: pltpu.VMEM(shape, dtype)
    dma = lambda n: pltpu.SemaphoreType.DMA((n,))
    scratch = [
        vmem((TILE, TILE)), vmem((TILE, TILE), jnp.int32), vmem(spectra.shape),
        *[vmem(t.shape, BF16) for t in tables],
        vmem((2, 64, 128)), vmem((2, 32, 128)),
        vmem((HALO, TILE)), vmem((2, 64, 128)), vmem((2, 32, 128)),
        vmem((HALF, TILE)), vmem((2, TILE, TILE), BF16),
        vmem((BAND, 2 * BAND)), vmem((BAND, 2 * BAND)),
        vmem((kernels, 2 * BAND, 2 * TILE), BF16), vmem((2, kernels, TILE, TILE)),
        vmem((2, HALF, TILE)), vmem((2, HALF, TILE)), vmem((HALF, TILE)), vmem((TILE, TILE)), vmem((TILE, TILE)), vmem((TILE, TILE)),
        vmem((kernels, 2 * TILE, TILE), BF16), vmem((BAND, 2 * BAND)), vmem((BAND, 2 * BAND)),
        vmem((HALO, TILE)), vmem((2, 64, 128)), vmem((2, 32, 128)),
        vmem((HALO, TILE)), vmem((2, 64, 128)), vmem((2, 32, 128)),
        vmem((HALF, TILE)),
        dma(7), dma(3), dma(5), dma(5), dma(6), dma(6), dma(5), dma(5),
    ]
    anywhere = pl.BlockSpec(memory_space=pl.ANY)
    outs = pl.pallas_call(
        body,
        out_shape=[jax.ShapeDtypeStruct((TILE, TILE), F32)] * 2,
        in_specs=[anywhere] * (3 + len(tables)),
        out_specs=[anywhere] * 2,
        scratch_shapes=scratch,
        compiler_params=pltpu.CompilerParams(
            collective_id=0, has_side_effects=True, vmem_limit_bytes=25165824
        ),
        name="socs_step",
    )(*[pltpu.with_memory_space_constraint(x, pltpu.HBM) for x in (mask, target, spectra, *map(jnp.asarray, tables))])

    def put(a, b, c, d, sem):
        copies = [pltpu.make_async_copy(a, c, sem.at[0]), pltpu.make_async_copy(b, d, sem.at[1])]
        for copy in copies:
            copy.start()
        for copy in copies:
            copy.wait()

    return pl.pallas_call(put, out_shape=[jax.ShapeDtypeStruct((TILE, TILE), F32)] * 2, name="put", in_specs=[anywhere] * 2, out_specs=[anywhere] * 2, scratch_shapes=[dma(2)], compiler_params=pltpu.CompilerParams(vmem_limit_bytes=4 * 1024 * 1024))(*outs)


def solution(mesh):
    return jax.shard_map(
        on_device,
        mesh=mesh,
        in_specs=(P("ty", "tx"), P("ty", "tx"), P(None, "kern", None, None)),
        out_specs=(P("ty", "tx"), P("ty", "tx")),
        check_vma=False,
    )
```
